32 devices in a mesh: groups: 2 (over x), frames: 16 (over z, y, core).
Axes of the slice: x: 2, y: 2, z: 4, core: 2. Of those that a mesh axis runs over, the one named last changes fastest.
Arguments:
- video: bfloat16 [4, 16, 128, 1024], P('groups', 'frames'), parts along dimension 0, may hold values from -70 to 70
- w_qkv: bfloat16 [1024, 3072], replicated, may hold values from -8 to 8
- w_out: bfloat16 [1024, 1024], replicated, may hold values from -0.1875 to 0.1875
- keep_list: int32 [4, 16, 128], P('groups', 'frames'), parts along dimension 0, may hold values from 0 to 127, each once within a row
- kept_counts: int32 [4, 16], P('groups', 'frames'), parts along dimension 0, may hold values from 1 to 4, 32 in all within a row
- w_proj: bfloat16 [1024, 8192], P(None, 'frames'), may hold values from -20 to 20
- llm_gain: bfloat16 [8192], P('frames'), may hold values from 0.099609375 to 1.8984375
- w_gate: bfloat16 [8192, 16384], P(None, 'frames'), may hold values from -0.0625 to 0.0625
- w_up: bfloat16 [8192, 16384], P(None, 'frames'), may hold values from -0.0625 to 0.0625
Outputs:
- llm_hidden: bfloat16 [4, 32, 16384], P('groups', None, 'frames'), parts along dimension 0
The draws below stay inside these ranges and needn't reach their ends.
There are 2 independent parts, one for each index of `groups`. The reference program is written for one: setup_inputs(seed, part) draws one part's arguments, and reference() takes and returns one part's arrays. A program takes and returns all parts, laid end to end along the dimension named above; an argument that names none is the same for every part. Nothing has to cross between parts.
Inputs may be any that keep to these rules, and one draw needn't show every extreme that they name: `keep_list`: each row of a frame lists every patch index once. `kept_counts`: the counts of one video sum to 32.
All inputs are finite; a program needn't handle non-finite values. No bound on the sum of `kept_counts` on one device may be relied on, other than what follows from the above.
Results may differ from the reference program's by a relative error of at most 0.0076.
Values may be sent and summed in bfloat16 or wider, within the bound.
No kernel may reach another device: no remote copies, remote signals or barrier semaphores. Data moves between devices by JAX's collectives and lax.ppermute only.
A program may use at most 128 MiB of HBM per device.

```python
import math
import jax
import jax.numpy as jnp
import numpy as np
from jax import lax

D = 1024
HEAD_DIM = 64
DL = 8192
FF = 16384
VIDEOS = 2
P_SIZE = 128
FRAMES = 16
KMAX = 4
SEQ = 32


def draw_video(key, part):
    full_shape = (VIDEOS, FRAMES, P_SIZE, D)
    base = jax.random.truncated_normal(key, -6.0, 6.0, full_shape, jnp.float32)
    return base.astype(jnp.bfloat16)


def draw_w_qkv(key, part):
    base = jax.random.truncated_normal(key, -6.0, 6.0, (D, 3 * D), jnp.float32) / math.sqrt(D)
    return jnp.clip(base, -8.0, 8.0).astype(jnp.bfloat16)


def draw_w_proj(key, part):
    base = jax.random.truncated_normal(key, -6.0, 6.0, (D, DL), jnp.float32) / math.sqrt(D)
    column = jnp.arange(DL, dtype=jnp.float32) / DL
    rise = jnp.exp(math.log(3.0) * column)
    spread = jnp.exp(jax.random.uniform(jax.random.fold_in(key, 14), (DL,), jnp.float32, 0.0, math.log(10.0)))
    return jnp.clip(base * (rise * spread)[None, :], -20.0, 20.0).astype(jnp.bfloat16)


def shard_levels(stream_key, shape, shards, low, high):
    def one(position, blocks):
        draws = jax.random.uniform(jax.random.fold_in(jax.random.fold_in(stream_key, 6), position), (blocks,), jnp.float32, low / len(shards), high / len(shards))
        return jnp.repeat(jnp.exp(draws), shape[position] // blocks).reshape((-1,) + (1,) * (len(shape) - position - 1))

    loudness = one(*shards[0])
    for cut in shards[1:]:
        loudness = loudness * one(*cut)
    return loudness


def split_up(amount, total, bound, slope):
    loads = [(1 << 20) // math.isqrt(standing ** slope) + 1 for standing in range(2, amount + 1)]
    rest, given = total - bound - (amount - 1), [1] * (amount - 1)
    while rest > 0:
        candidates = [i for i in range(amount - 1) if given[i] < bound]
        pool, budget = sum([loads[i] for i in candidates]), rest
        for i in candidates:
            more = min(bound - given[i], max(1, budget * loads[i] // pool), rest)
            given[i] = given[i] + more
            rest = rest - more
    return np.array([bound] + given)


def ragged_sizes(own_key, count, total, reach, skew):
    if count == 2:
        one = jax.random.randint(own_key, (), max(1, total - reach), min(reach, total - 1) + 1)
        return jnp.stack([one, total - one])
    lengths = jnp.asarray(split_up(count, total, reach, skew), jnp.int32)
    pairs = (count - 1) // 2
    donor, sink = lengths[1:1 + 2 * pairs:2], lengths[2:2 + 2 * pairs:2]
    room = jnp.minimum(donor - 1, reach - sink)
    shifted = jax.random.randint(jax.random.fold_in(own_key, 1), (pairs,), 0, 1 << 20) % (room + 1)
    lengths = lengths.at[1:1 + 2 * pairs:2].set(donor - shifted).at[2:2 + 2 * pairs:2].set(sink + shifted)
    return lengths[jax.random.permutation(jax.random.fold_in(own_key, 2), count)]


def bell_draw(key, dims, width, most, pieces=(), kind=jnp.bfloat16):
    drawn = width * jax.random.normal(key, dims, jnp.float32)
    if pieces:
        drawn = drawn * shard_levels(key, dims, pieces, -0.22, 0.18)
    return jnp.clip(drawn, -most, most).astype(kind)


def setup_inputs(seed: int = 0, part: int = 0) -> dict:
    splits = jax.random.split(jax.random.key(seed), 10)
    part_splits = jax.random.split(jax.random.fold_in(splits[9], part), 10)
    return {
        "video": draw_video(jax.random.fold_in(jax.random.fold_in(splits[9], part), 71), part),
        "w_qkv": draw_w_qkv(jax.random.fold_in(splits[9], 71), part),
        "w_out": bell_draw(splits[2], (D, D), D ** -0.5, 0.1875),
        "keep_list": jax.vmap(lambda own: jax.random.permutation(own, P_SIZE))(jax.random.split(part_splits[3], VIDEOS * FRAMES)).reshape((VIDEOS, FRAMES, P_SIZE)).astype(jnp.int32),
        "kept_counts": jax.vmap(lambda own: ragged_sizes(own, FRAMES, SEQ, KMAX, 2))(jax.random.split(part_splits[4], VIDEOS)).reshape((VIDEOS, FRAMES)).astype(jnp.int32),
        "w_proj": draw_w_proj(jax.random.fold_in(splits[9], 71), part),
        "llm_gain": jnp.clip(1.0 + 0.18 * jax.random.normal(splits[6], (DL,), jnp.float32), 0.099609375, 1.8984375).astype(jnp.bfloat16),
        "w_gate": bell_draw(splits[7], (DL, FF), DL ** -0.5, 0.0625, ((1, 16),)),
        "w_up": bell_draw(splits[8], (DL, FF), DL ** -0.5, 0.0625, ((1, 16),)),
    }


NORM_EPS = 1e-05
SCORE_SCALE = 0.125

def layer_norm(values):
    floated = values.astype(jnp.float32)
    average = lax.optimization_barrier(jnp.mean(floated, axis=-1, keepdims=True))
    centred = floated - average
    variance = lax.optimization_barrier(jnp.mean(centred * centred, axis=-1, keepdims=True))
    return (centred * lax.rsqrt(variance + NORM_EPS)).astype(jnp.bfloat16)

def sequence_slots(counts, seq_len, slot_width):
    counts = counts.astype(jnp.int32)
    offsets = (jnp.cumsum(counts, axis=1) - counts).astype(jnp.int32)
    positions = lax.broadcasted_iota(jnp.int32, (counts.shape[0], seq_len), 1)
    started = (offsets[:, None, :] <= positions[:, :, None]).astype(jnp.int32)
    owner_frame = (lax.optimization_barrier(jnp.sum(started, axis=2)) - 1).astype(jnp.int32)
    frame_ids = lax.broadcasted_iota(jnp.int32, started.shape, 2)
    begin_at = lax.optimization_barrier(jnp.sum(jnp.where(frame_ids == owner_frame[:, :, None], offsets[:, None, :], 0), axis=2)).astype(jnp.int32)
    return (owner_frame * slot_width + positions - begin_at).astype(jnp.int32)

def temporal_attention(queries, keys_in, values_in):
    scores = jnp.einsum('fphe,gphe->phfg', queries.astype(jnp.float32), keys_in.astype(jnp.float32)) * SCORE_SCALE
    largest = lax.optimization_barrier(jnp.max(scores, axis=-1, keepdims=True))
    weights_exp = jnp.exp(scores - largest)
    weights = (weights_exp / lax.optimization_barrier(jnp.sum(weights_exp, axis=-1, keepdims=True))).astype(jnp.bfloat16)
    return jnp.einsum('phfg,gphe->fphe', weights.astype(jnp.float32), values_in.astype(jnp.float32)).astype(jnp.bfloat16)

def take_frame_rows(frame_rows, picks_row):
    return jnp.take(frame_rows, picks_row, axis=0)

def one_video(video_frames, keep_rows, count_row, w_qkv, w_out, w_proj, llm_gain, w_gate, w_up):
    frame_count, patch_count, model_width = video_frames.shape
    head_count = model_width // HEAD_DIM
    normed = layer_norm(video_frames)
    projected = jnp.dot(normed.reshape(-1, model_width), w_qkv, preferred_element_type=jnp.float32).astype(jnp.bfloat16)
    projected = projected.reshape(frame_count, patch_count, 3, head_count, HEAD_DIM)
    attended = temporal_attention(projected[:, :, 0], projected[:, :, 1], projected[:, :, 2])
    attended = attended.reshape(-1, model_width)
    encoded = (video_frames.astype(jnp.float32).reshape(-1, model_width) + jnp.dot(attended, w_out, preferred_element_type=jnp.float32)).astype(jnp.bfloat16)
    encoded = encoded.reshape(frame_count, patch_count, model_width)
    slot_rows = jax.vmap(take_frame_rows)(encoded, keep_rows[:, :KMAX].astype(jnp.int32))
    slot_rows = slot_rows.reshape(-1, model_width)
    sequence_order = sequence_slots(count_row[None, :], SEQ, KMAX)[0]
    token_rows = jnp.take(slot_rows, sequence_order, axis=0)
    projected_rows = jnp.dot(token_rows, w_proj, preferred_element_type=jnp.float32)
    mean_square = lax.optimization_barrier(jnp.mean(projected_rows * projected_rows, axis=1, keepdims=True))
    normed_rows = (projected_rows * lax.rsqrt(mean_square + NORM_EPS) * llm_gain.astype(jnp.float32)).astype(jnp.bfloat16)
    gate_sum = jnp.dot(normed_rows, w_gate, preferred_element_type=jnp.float32)
    upward = jnp.dot(normed_rows, w_up, preferred_element_type=jnp.float32)
    return (jax.nn.silu(gate_sum) * upward).astype(jnp.bfloat16)

def reference(video, w_qkv, w_out, keep_list, kept_counts, w_proj, llm_gain, w_gate, w_up):

    def run_video(inputs):
        return one_video(inputs[0], inputs[1], inputs[2], w_qkv, w_out, w_proj, llm_gain, w_gate, w_up)
    return lax.map(run_video, (video, keep_list, kept_counts))
```

```python
import functools

import jax
import jax.numpy as jnp
from jax import lax
from jax.experimental import pallas as pl
from jax.experimental.pallas import tpu as pltpu
from jax.sharding import Mesh
from jax.sharding import PartitionSpec as P

HEAD_DIM = 64
TOKL = 2
KMAX = 4
LANES = 128
NORM_EPS = 1e-05
SCORE_SCALE = 0.125
MIB = 1 << 20
F32 = jnp.float32
BF16 = jnp.bfloat16


def dot32(left, right):
    return jnp.dot(left, right, preferred_element_type=F32)


def swap_halves(values):
    rows = values.shape[-2] // 2
    return jnp.concatenate([values[..., rows:, :], values[..., :rows, :]], axis=-2)


def whole(space=pltpu.VMEM):
    return pl.BlockSpec(memory_space=space)


def params(limit):
    return pltpu.CompilerParams(vmem_limit_bytes=int(limit))


def index_kernel(counts_ref, keep_ref, gain_ref, out_ref):
    videos = keep_ref.shape[0]
    lane = lax.broadcasted_iota(jnp.int32, (1, LANES), 1)
    rows = []
    for v in range(videos):
        listed = keep_ref[v, :, :LANES].astype(F32)
        rows.append(jnp.where(lane == KMAX, counts_ref[v, 0].astype(F32), listed))
    gain = gain_ref[...].astype(F32)
    width = gain.shape[1]
    for start in range(0, width, LANES):
        piece = gain[:, start : start + LANES]
        if piece.shape[1] < LANES:
            piece = jnp.concatenate([piece, jnp.ones((1, LANES - piece.shape[1]), F32)], axis=1)
        rows.append(piece)
    while len(rows) < out_ref.shape[1]:
        rows.append(jnp.zeros((1, LANES), F32))
    message = jnp.concatenate(rows, axis=0)
    out_ref[...] = jnp.broadcast_to(message[None], out_ref.shape)


def select_kernel(index_ref, video_ref, out_ref):
    frames = index_ref.shape[0]
    videos, _, patches, width = video_ref.shape
    seq = frames * TOKL
    half = width // 2
    own = out_ref.shape[1] // 2
    row = lax.broadcasted_iota(jnp.int32, (frames, frames), 0)
    col = lax.broadcasted_iota(jnp.int32, (frames, frames), 1)
    before = (col < row).astype(BF16)
    token = lax.broadcasted_iota(jnp.int32, (frames, seq), 1)
    patch = lax.broadcasted_iota(jnp.int32, (frames, patches), 1).astype(F32)
    for v in range(videos):
        table = index_ref[:, v, :]
        count = table[:, KMAX : KMAX + 1]
        offset = dot32(before, jnp.broadcast_to(count, (frames, LANES)).astype(BF16))[:, :1]
        place = token.astype(F32) - offset
        at_token, at_patch = [], []
        for s in range(KMAX):
            live = jnp.logical_and(place == s, count > s)
            at_token.append(jnp.where(live, 1.0, 0.0))
            at_patch.append(jnp.where(table[:, s : s + 1] == patch, 1.0, 0.0))
        at_token = jnp.concatenate(at_token, axis=0).astype(BF16)
        at_patch = jnp.concatenate(at_patch, axis=0).astype(BF16)
        chosen = lax.dot_general(
            at_token, at_patch, (((0,), (0,)), ((), ())), preferred_element_type=F32
        ).astype(BF16)
        taken = dot32(chosen, video_ref[v, 0]).astype(BF16)
        base = v * seq
        for peer in range(base // own, (base + seq) // own):
            first = peer * own - base
            rows = taken[first : first + own]
            out_ref[peer] = jnp.concatenate([rows[:, :half], rows[:, half:]], axis=0)


def attend_kernel(me_ref, index_ref, rows_ref, w_qkv_ref, w_out_ref, out_ref):
    frames, packed, half = rows_ref.shape
    own = packed // 2
    width = 2 * half
    heads = width // HEAD_DIM
    seq = frames * TOKL
    videos = frames * own // seq
    raw = rows_ref[...].astype(F32)

    def feature_mean(values):
        part = jnp.sum(values, axis=-1, keepdims=True)
        return (part + swap_halves(part)) / width

    centred = raw - feature_mean(raw)
    variance = feature_mean(centred * centred)
    normed = (centred * lax.rsqrt(variance + NORM_EPS)).astype(BF16).reshape(-1, half)

    def project(start):
        low = dot32(normed, w_qkv_ref[:half, start : start + width])
        high = dot32(normed, w_qkv_ref[half:, start : start + width])
        low = low.reshape(frames, packed, width)
        high = high.reshape(frames, packed, width)
        return (low + swap_halves(high)).astype(BF16).astype(F32)

    table = index_ref[...]
    row = lax.broadcasted_iota(jnp.int32, (1, packed, 1), 1)
    flat = me_ref[0] * own + jnp.where(row >= own, row - own, row)
    owner = jnp.zeros((frames, packed, 1), jnp.bool_)
    for v in range(videos):
        count = table[:, v : v + 1, KMAX : KMAX + 1]
        upto = count
        step = 1
        while step < frames:
            moved = jnp.concatenate([jnp.zeros((step, 1, 1), F32), upto[:-step]], axis=0)
            upto = upto + moved
            step *= 2
        place = (flat - v * seq).astype(F32)
        inside = jnp.logical_and(place >= upto - count, place < upto)
        ours = jnp.logical_and(flat >= v * seq, flat < (v + 1) * seq)
        owner = jnp.logical_or(owner, jnp.logical_and(inside, ours))

    def of_owner(values):
        return jnp.sum(jnp.where(owner, values, 0.0), axis=0)

    query = of_owner(project(0))
    product = (project(width) * query[None]).reshape(-1, width)
    feature = lax.broadcasted_iota(jnp.int32, (width, LANES), 0) // HEAD_DIM
    head = lax.broadcasted_iota(jnp.int32, (width, LANES), 1)
    to_head = jnp.where(feature == head, 1.0, 0.0).astype(BF16)
    coarse = product.astype(BF16)
    rest = product - coarse.astype(F32)
    fine = rest.astype(BF16)
    last = (rest - fine.astype(F32)).astype(BF16)
    scores = dot32(coarse, to_head) + dot32(fine, to_head) + dot32(last, to_head)
    scores = scores.reshape(frames, packed, LANES) * SCORE_SCALE
    raised = jnp.exp(scores - jnp.max(scores, axis=0, keepdims=True))
    weights = (raised / jnp.sum(raised, axis=0, keepdims=True)).astype(BF16)
    head = lax.broadcasted_iota(jnp.int32, (LANES, width), 0)
    feature = lax.broadcasted_iota(jnp.int32, (LANES, width), 1) // HEAD_DIM
    from_head = jnp.where(feature == head, 1.0, 0.0).astype(BF16)
    spread = dot32(weights.reshape(-1, LANES), from_head).reshape(frames, packed, width)
    attended = jnp.sum(spread * project(2 * width), axis=0).astype(BF16)
    change = dot32(attended, w_out_ref[...])
    place = lax.broadcasted_iota(jnp.int32, (packed, half), 0)
    change = jnp.where(place < own, change[:, :half], swap_halves(change[:, half:]))
    encoded = (of_owner(raw) + change).astype(BF16)
    out_ref[...] = jnp.broadcast_to(encoded[None], out_ref.shape)


def project_kernel(rows_ref, w_proj_ref, gain_ref, out_ref):
    frames, packed, half = rows_ref.shape
    own = packed // 2
    tokens = frames * own
    columns = w_proj_ref.shape[1]
    rows = rows_ref[...].reshape(frames * packed, half)
    token = lax.broadcasted_iota(jnp.int32, (tokens, frames * packed), 0)
    source = lax.broadcasted_iota(jnp.int32, (tokens, frames * packed), 1)
    first = (token // own) * packed + token % own
    low = dot32(jnp.where(source == first, 1.0, 0.0).astype(BF16), rows).astype(BF16)
    high = dot32(jnp.where(source == first + own, 1.0, 0.0).astype(BF16), rows).astype(BF16)
    total = dot32(low, w_proj_ref[:half, :]) + dot32(high, w_proj_ref[half:, :])
    gained = (total * gain_ref[...].astype(F32)).astype(BF16)
    out_ref[...] = jnp.broadcast_to(gained[None], out_ref.shape)


def hidden_kernel(index_ref, rows_ref, w_gate_ref, w_up_ref, out_ref, joined):
    cores, chips, tokens, columns = rows_ref.shape
    depth = cores * chips * columns
    first = index_ref.shape[1]
    gain_rows = -(-columns // LANES)
    videos = out_ref.shape[0]
    squares = jnp.zeros((tokens, 1), F32)
    for chip in range(chips):
        for core in range(cores):
            place = chip * cores + core
            piece = rows_ref[core, chip]
            joined[:, place * columns : (place + 1) * columns] = piece
            for r in range(gain_rows):
                part = piece[:, r * LANES : (r + 1) * LANES].astype(F32)
                gain = index_ref[place, videos + r : videos + r + 1, : part.shape[1]]
                part = part / gain
                squares = squares + jnp.sum(part * part, axis=1, keepdims=True)
    scale = lax.rsqrt(squares / depth + NORM_EPS)
    width = out_ref.shape[2]
    block = min(width, 256)

    for start in range(0, width, block):
        gate = dot32(joined[...], w_gate_ref[:, start : start + block]) * scale
        up = dot32(joined[...], w_up_ref[:, start : start + block]) * scale
        hidden = (jax.nn.silu(gate) * up).astype(BF16)
        out_ref[:, :, start : start + block] = hidden.reshape(videos, -1, block)


def local(video, w_qkv, w_out, keep_list, kept_counts, w_proj, llm_gain, w_gate, w_up):
    videos, _, patches, width = video.shape
    chips, cores = lax.axis_size("chips"), lax.axis_size("cores")
    frames = chips * cores
    axes = ("chips", "cores")
    seq = frames * TOKL
    tokens = videos * seq
    packed = 2 * (tokens // frames)
    half = width // 2
    columns = w_proj.shape[1]
    me = lax.axis_index(axes).astype(jnp.int32).reshape(1)
    spread = functools.partial(lax.all_to_all, split_axis=0, concat_axis=0, tiled=True)

    message_rows = -(-(videos + -(-columns // LANES)) // 8) * 8
    message = pl.pallas_call(
        index_kernel,
        out_shape=jax.ShapeDtypeStruct((frames, message_rows, LANES), F32),
        in_specs=[whole(pltpu.SMEM), whole(), whole()],
        out_specs=whole(),
        compiler_params=params(2 * MIB),
        name="index",
    )(kept_counts, keep_list, llm_gain.reshape(1, -1))
    index = spread(message, axes)

    chosen = pl.pallas_call(
        select_kernel,
        out_shape=jax.ShapeDtypeStruct((frames, packed, half), BF16),
        in_specs=[whole(), whole()],
        out_specs=whole(),
        compiler_params=params(4 * MIB + 8 * tokens * width),
        name="select",
    )(index, video)
    seen = spread(chosen, axes)

    encoded = pl.pallas_call(
        attend_kernel,
        out_shape=jax.ShapeDtypeStruct((frames, packed, half), BF16),
        in_specs=[whole(pltpu.SMEM), whole(), whole(), whole(), whole()],
        out_specs=whole(),
        compiler_params=params(12 * MIB + 24 * frames * packed * width),
        name="attend",
    )(me, index, seen, w_qkv, w_out)
    token_rows = spread(encoded, axes)

    gained = pl.pallas_call(
        project_kernel,
        out_shape=jax.ShapeDtypeStruct((chips, tokens, columns), BF16),
        in_specs=[whole(), whole(), whole()],
        out_specs=whole(),
        compiler_params=params(6 * MIB + 4 * tokens * chips * columns),
        name="project",
    )(token_rows, w_proj, llm_gain.reshape(1, -1))
    mine = spread(gained, "chips")
    rows = lax.all_gather(mine, "cores", axis=0)

    return pl.pallas_call(
        hidden_kernel,
        out_shape=jax.ShapeDtypeStruct((videos, seq, w_gate.shape[1]), BF16),
        in_specs=[whole(), whole(), whole(), whole()],
        out_specs=whole(),
        scratch_shapes=[pltpu.VMEM((tokens, w_gate.shape[0]), BF16)],
        compiler_params=params(52 * MIB),
        name="hidden",
    )(index, rows, w_gate, w_up)


def solution(mesh):
    groups, frames = mesh.devices.shape
    cores = 2 if frames % 2 == 0 else 1
    split = Mesh(mesh.devices.reshape(groups, frames // cores, cores), ("groups", "chips", "cores"))
    spread = ("chips", "cores")
    in_specs = (
        P("groups", spread, None, None),
        P(),
        P(),
        P("groups", spread, None),
        P("groups", spread),
        P(None, spread),
        P(spread),
        P(None, spread),
        P(None, spread),
    )
    out_specs = P("groups", None, spread)
    return jax.shard_map(local, mesh=split, in_specs=in_specs, out_specs=out_specs, check_vma=False)
```

```python
import functools

import jax
import jax.numpy as jnp
from jax import lax
from jax.experimental import pallas as pl
from jax.experimental.pallas import tpu as pltpu
from jax.sharding import Mesh
from jax.sharding import PartitionSpec as P

HEAD_DIM = 64
TOKL = 2
KMAX = 4
LANES = 128
NORM_EPS = 1e-05
SCORE_SCALE = 0.125
MIB = 1 << 20
F32 = jnp.float32
BF16 = jnp.bfloat16


def dot32(left, right):
    return jnp.dot(left, right, preferred_element_type=F32)


def swap_halves(values):
    rows = values.shape[-2] // 2
    return jnp.concatenate([values[..., rows:, :], values[..., :rows, :]], axis=-2)


def whole(space=pltpu.VMEM):
    return pl.BlockSpec(memory_space=space)


def params(limit):
    return pltpu.CompilerParams(vmem_limit_bytes=int(limit))


def index_kernel(me_ref, counts_ref, keep_ref, gain_ref, out_ref):
    del me_ref
    videos = keep_ref.shape[0]
    lane = lax.broadcasted_iota(jnp.int32, (1, LANES), 1)
    rows = []
    for v in range(videos):
        listed = keep_ref[v, :, :LANES].astype(F32)
        rows.append(jnp.where(lane == KMAX, counts_ref[0, v].astype(F32), listed))
    gain = gain_ref[...].astype(F32)
    if gain.shape[1] < LANES:
        fill = jnp.ones((gain.shape[0], LANES - gain.shape[1]), F32)
        gain = jnp.concatenate([gain, fill], axis=1)
    rows.append(gain)
    spare = out_ref.shape[1] - videos - gain.shape[0]
    if spare:
        rows.append(jnp.zeros((spare, LANES), F32))
    message = jnp.concatenate(rows, axis=0)
    out_ref[...] = jnp.broadcast_to(message[None], out_ref.shape)


def select_kernel(index_ref, video_ref, out_ref):
    frames = index_ref.shape[0]
    videos, _, patches, width = video_ref.shape
    seq = frames * TOKL
    half = width // 2
    own = out_ref.shape[1] // 2
    row = lax.broadcasted_iota(jnp.int32, (frames, frames), 0)
    col = lax.broadcasted_iota(jnp.int32, (frames, frames), 1)
    before = (col < row).astype(BF16)
    token = lax.broadcasted_iota(jnp.int32, (frames, seq), 1)
    patch = lax.broadcasted_iota(jnp.int32, (frames, patches), 1).astype(F32)
    for v in range(videos):
        table = index_ref[:, v, :]
        count = table[:, KMAX : KMAX + 1]
        offset = dot32(before, jnp.broadcast_to(count, (frames, LANES)).astype(BF16))[:, :1]
        place = token.astype(F32) - offset
        at_token, at_patch = [], []
        for s in range(KMAX):
            live = jnp.logical_and(place == s, count > s)
            at_token.append(jnp.where(live, 1.0, 0.0))
            at_patch.append(jnp.where(table[:, s : s + 1] == patch, 1.0, 0.0))
        at_token = jnp.concatenate(at_token, axis=0).astype(BF16)
        at_patch = jnp.concatenate(at_patch, axis=0).astype(BF16)
        chosen = lax.dot_general(
            at_token, at_patch, (((0,), (0,)), ((), ())), preferred_element_type=F32
        ).astype(BF16)
        taken = dot32(chosen, video_ref[v, 0]).astype(BF16)
        base = v * seq
        for peer in range(base // own, (base + seq) // own):
            first = peer * own - base
            rows = taken[first : first + own]
            out_ref[peer] = jnp.concatenate([rows[:, :half], rows[:, half:]], axis=0)


def attend_kernel(me_ref, index_ref, rows_ref, w_qkv_ref, w_out_ref, out_ref):
    frames, packed, half = rows_ref.shape
    own = packed // 2
    width = 2 * half
    heads = width // HEAD_DIM
    seq = frames * TOKL
    videos = frames * own // seq
    raw = rows_ref[...].astype(F32)

    def feature_mean(values):
        part = jnp.sum(values, axis=-1, keepdims=True)
        return (part + swap_halves(part)) / width

    centred = raw - feature_mean(raw)
    variance = feature_mean(centred * centred)
    normed = (centred * lax.rsqrt(variance + NORM_EPS)).astype(BF16).reshape(-1, half)

    def project(start):
        low = dot32(normed, w_qkv_ref[:half, start : start + width])
        high = dot32(normed, w_qkv_ref[half:, start : start + width])
        low = low.reshape(frames, packed, width)
        high = high.reshape(frames, packed, width)
        return (low + swap_halves(high)).astype(BF16).astype(F32)

    table = index_ref[...]
    row = lax.broadcasted_iota(jnp.int32, (1, packed, 1), 1)
    flat = me_ref[0] * own + jnp.where(row >= own, row - own, row)
    owner = jnp.zeros((frames, packed, 1), jnp.bool_)
    for v in range(videos):
        count = table[:, v : v + 1, KMAX : KMAX + 1]
        upto = count
        step = 1
        while step < frames:
            moved = jnp.concatenate([jnp.zeros((step, 1, 1), F32), upto[:-step]], axis=0)
            upto = upto + moved
            step *= 2
        place = (flat - v * seq).astype(F32)
        inside = jnp.logical_and(place >= upto - count, place < upto)
        ours = jnp.logical_and(flat >= v * seq, flat < (v + 1) * seq)
        owner = jnp.logical_or(owner, jnp.logical_and(inside, ours))

    def of_owner(values):
        return jnp.sum(jnp.where(owner, values, 0.0), axis=0)

    query = of_owner(project(0))
    product = (project(width) * query[None]).reshape(-1, width)
    feature = lax.broadcasted_iota(jnp.int32, (width, LANES), 0) // HEAD_DIM
    head = lax.broadcasted_iota(jnp.int32, (width, LANES), 1)
    to_head = jnp.where(feature == head, 1.0, 0.0).astype(BF16)
    coarse = product.astype(BF16)
    rest = product - coarse.astype(F32)
    fine = rest.astype(BF16)
    last = (rest - fine.astype(F32)).astype(BF16)
    scores = dot32(coarse, to_head) + dot32(fine, to_head) + dot32(last, to_head)
    scores = scores.reshape(frames, packed, LANES) * SCORE_SCALE
    raised = jnp.exp(scores - jnp.max(scores, axis=0, keepdims=True))
    weights = (raised / jnp.sum(raised, axis=0, keepdims=True)).astype(BF16)
    head = lax.broadcasted_iota(jnp.int32, (LANES, width), 0)
    feature = lax.broadcasted_iota(jnp.int32, (LANES, width), 1) // HEAD_DIM
    from_head = jnp.where(feature == head, 1.0, 0.0).astype(BF16)
    spread = dot32(weights.reshape(-1, LANES), from_head).reshape(frames, packed, width)
    attended = jnp.sum(spread * project(2 * width), axis=0).astype(BF16)
    change = dot32(attended, w_out_ref[...])
    place = lax.broadcasted_iota(jnp.int32, (packed, half), 0)
    change = jnp.where(place < own, change[:, :half], swap_halves(change[:, half:]))
    encoded = (of_owner(raw) + change).astype(BF16)
    out_ref[...] = jnp.broadcast_to(encoded[None], out_ref.shape)


def project_kernel(rows_ref, w_proj_ref, gain_ref, out_ref):
    frames, packed, half = rows_ref.shape
    own = packed // 2
    tokens = frames * own
    rows = rows_ref[...].reshape(frames * packed, half)
    token = lax.broadcasted_iota(jnp.int32, (tokens, frames * packed), 0)
    source = lax.broadcasted_iota(jnp.int32, (tokens, frames * packed), 1)
    first = (token // own) * packed + token % own
    low = dot32(jnp.where(source == first, 1.0, 0.0).astype(BF16), rows).astype(BF16)
    high = dot32(jnp.where(source == first + own, 1.0, 0.0).astype(BF16), rows).astype(BF16)
    total = dot32(low, w_proj_ref[:half, :]) + dot32(high, w_proj_ref[half:, :])
    gain = gain_ref[...].astype(F32)
    lanes = gain.shape[1]
    for r in range(gain.shape[0]):
        piece = slice(r * lanes, (r + 1) * lanes)
        gained = (total[:, piece] * gain[r : r + 1]).astype(BF16)
        out_ref[:, :, piece] = jnp.broadcast_to(gained[None], (out_ref.shape[0], tokens, lanes))


def products(core, videos, index_ref, rows_ref, w_gate_ref, w_up_ref, gate_in, up_in, emit):
    chips, tokens, columns = rows_ref.shape
    cores = index_ref.shape[0] // chips
    gain_rows = -(-columns // LANES)
    squares = jnp.zeros((tokens, LANES), F32)
    for chip in range(chips):
        gains = index_ref[chip * cores + core, videos : videos + gain_rows, :]
        for r in range(gain_rows):
            part = rows_ref[chip, :, r * LANES : min((r + 1) * LANES, columns)].astype(F32)
            part = part / gains[r : r + 1, : part.shape[1]]
            part = part * part
            if part.shape[1] < LANES:
                fill = jnp.zeros((tokens, LANES - part.shape[1]), F32)
                part = jnp.concatenate([part, fill], axis=1)
            squares = squares + part
    width = w_gate_ref.shape[1]
    block = min(width, 256)
    for first in range(0, width, block):
        sums = []
        for w_ref, begin_ref in ((w_gate_ref, gate_in), (w_up_ref, up_in)):
            total = None if begin_ref is None else begin_ref[:, first : first + block]
            for chip in range(chips):
                depth = pl.ds(pl.multiple_of((chip * cores + core) * columns, columns), columns)
                part = dot32(rows_ref[chip], w_ref[depth, first : first + block])
                total = part if total is None else total + part
            sums.append(total)
        emit(first, block, *sums)
    return squares


def first_kernel(
    videos, me_ref, index_ref, rows_ref, w_gate_ref, w_up_ref, gate_ref, up_ref, squares_ref
):
    def emit(first, block, gate, up):
        gate_ref[:, first : first + block] = gate
        up_ref[:, first : first + block] = up

    core = lax.rem(me_ref[0], index_ref.shape[0] // rows_ref.shape[0])
    squares_ref[...] = products(
        core, videos, index_ref, rows_ref, w_gate_ref, w_up_ref, None, None, emit
    )


def second_kernel(
    me_ref, index_ref, rows_ref, w_gate_ref, w_up_ref, gate_ref, up_ref, squares_ref, out_ref,
    gate_sum, up_sum,
):
    videos = out_ref.shape[0]

    def emit(first, block, gate, up):
        gate_sum[:, first : first + block] = gate
        up_sum[:, first : first + block] = up

    cores = index_ref.shape[0] // rows_ref.shape[0]
    core = cores - 1 - lax.rem(me_ref[0], cores)
    squares = squares_ref[...] + products(
        core, videos, index_ref, rows_ref, w_gate_ref, w_up_ref, gate_ref, up_ref, emit
    )
    mean = jnp.sum(squares, axis=1, keepdims=True) / w_gate_ref.shape[0]
    scale = lax.rsqrt(mean + NORM_EPS)
    hidden = jax.nn.silu(gate_sum[...] * scale) * (up_sum[...] * scale)
    out_ref[...] = hidden.astype(BF16).reshape(out_ref.shape)


def local(video, w_qkv, w_out, keep_list, kept_counts, w_proj, llm_gain, w_gate, w_up):
    videos, _, patches, width = video.shape
    chips, cores = lax.axis_size("chips"), lax.axis_size("cores")
    frames = chips * cores
    axes = ("chips", "cores")
    seq = frames * TOKL
    tokens = videos * seq
    packed = 2 * (tokens // frames)
    half = width // 2
    columns = w_proj.shape[1]
    me = lax.axis_index(axes).astype(jnp.int32).reshape(1)
    spread = functools.partial(lax.all_to_all, split_axis=0, concat_axis=0, tiled=True)
    gain_rows = -(-columns // LANES)
    gain = llm_gain.reshape(gain_rows, -1)

    message = pl.pallas_call(
        index_kernel,
        out_shape=jax.ShapeDtypeStruct((frames, -(-(videos + gain_rows) // 8) * 8, LANES), F32),
        in_specs=[whole(pltpu.SMEM), whole(pltpu.SMEM), whole(), whole()],
        out_specs=whole(),
        compiler_params=params(2 * MIB),
        cost_estimate=pl.CostEstimate(flops=20000000000, bytes_accessed=65536, transcendentals=0),
        name="index",
    )(me, kept_counts.T, keep_list, gain)
    index = spread(message, axes)

    chosen = pl.pallas_call(
        select_kernel,
        out_shape=jax.ShapeDtypeStruct((frames, packed, half), BF16),
        in_specs=[whole(), whole()],
        out_specs=whole(),
        compiler_params=params(3 * MIB + 8 * tokens * width),
        name="select",
    )(index, video)
    seen = spread(chosen, axes)

    encoded = pl.pallas_call(
        attend_kernel,
        out_shape=jax.ShapeDtypeStruct((frames, packed, half), BF16),
        in_specs=[whole(pltpu.SMEM), whole(), whole(), whole(), whole()],
        out_specs=whole(),
        compiler_params=params(4 * MIB + 24 * frames * packed * width),
        name="attend",
    )(me, index, seen, w_qkv, w_out)
    token_rows = spread(encoded, axes)

    gained = pl.pallas_call(
        project_kernel,
        out_shape=jax.ShapeDtypeStruct((chips, tokens, columns), BF16),
        in_specs=[whole(), whole(), whole()],
        out_specs=whole(),
        compiler_params=params(4 * MIB + 4 * tokens * chips * columns),
        name="project",
    )(token_rows, w_proj, gain)
    mine = spread(gained, "chips")
    theirs = lax.ppermute(mine, "cores", [(0, 1), (1, 0)])

    units = w_gate.shape[1]
    part = jax.ShapeDtypeStruct((tokens, units), F32)
    work = pl.CostEstimate(
        flops=2 * tokens * w_gate.shape[0] * units,
        bytes_accessed=2 * w_gate.shape[0] * units,
        transcendentals=0,
    )
    begun = pl.pallas_call(
        functools.partial(first_kernel, videos),
        out_shape=(part, part, jax.ShapeDtypeStruct((tokens, LANES), F32)),
        in_specs=[whole(pltpu.SMEM)] + [whole()] * 4,
        out_specs=(whole(), whole(), whole()),
        compiler_params=params(4 * MIB + 16 * tokens * units),
        cost_estimate=work,
        name="first",
    )(me, index, mine, w_gate, w_up)
    return pl.pallas_call(
        second_kernel,
        out_shape=jax.ShapeDtypeStruct((videos, seq, units), BF16),
        in_specs=[whole(pltpu.SMEM)] + [whole()] * 7,
        out_specs=whole(),
        scratch_shapes=[pltpu.VMEM((tokens, units), F32)] * 2,
        compiler_params=params(4 * MIB + 24 * tokens * units),
        cost_estimate=work,
        name="second",
    )(me, index, theirs, w_gate, w_up, *begun)


def solution(mesh):
    groups, frames = mesh.devices.shape
    cores = 2
    split = Mesh(mesh.devices.reshape(groups, frames // cores, cores), ("groups", "chips", "cores"))
    spread = ("chips", "cores")
    in_specs = (
        P("groups", spread, None, None),
        P(),
        P(),
        P("groups", spread, None),
        P("groups", spread),
        P(None, spread),
        P(spread),
        P(None, spread),
        P(None, spread),
    )
    out_specs = P("groups", None, spread)
    return jax.shard_map(local, mesh=split, in_specs=in_specs, out_specs=out_specs, check_vma=False)
```

```python
import functools

import jax
import jax.numpy as jnp
from jax import lax
from jax.experimental import pallas as pl
from jax.experimental.pallas import tpu as pltpu
from jax.sharding import Mesh
from jax.sharding import PartitionSpec as P

HEAD_DIM = 64
TOKL = 2
KMAX = 4
LANES = 128
NORM_EPS = 1e-05
SCORE_SCALE = 0.125
DIRECT = 4
MIB = 1 << 20
COVER_FLOPS = 20_000_000_000
F32 = jnp.float32
BF16 = jnp.bfloat16


def dot32(left, right):
    return jnp.dot(left, right, preferred_element_type=F32)


def swap_halves(values):
    rows = values.shape[-2] // 2
    return jnp.concatenate([values[..., rows:, :], values[..., :rows, :]], axis=-2)


def whole(space=pltpu.VMEM):
    return pl.BlockSpec(memory_space=space)


def params(limit):
    return pltpu.CompilerParams(vmem_limit_bytes=int(limit))


def collect_kernel(counts_hbm, keep_hbm, gain_hbm, out_ref, counts_ref, keep_ref, gain_ref, sems):
    arrays = ((counts_hbm, counts_ref), (keep_hbm, keep_ref), (gain_hbm, gain_ref))
    copies = [
        pltpu.make_async_copy(source, target, sems.at[i])
        for i, (source, target) in enumerate(arrays)
    ]
    for copy in copies:
        copy.start()
    for copy in copies:
        copy.wait()
    videos = keep_ref.shape[0]
    lane = lax.broadcasted_iota(jnp.int32, (1, LANES), 1)
    counts = counts_ref[...].astype(F32)
    rows = []
    for v in range(videos):
        listed = keep_ref[v, :, :LANES].astype(F32)
        rows.append(jnp.where(lane == KMAX, counts[:, v : v + 1], listed))
    gain = gain_ref[...].astype(F32)
    if gain.shape[1] < LANES:
        fill = jnp.ones((gain.shape[0], LANES - gain.shape[1]), F32)
        gain = jnp.concatenate([gain, fill], axis=1)
    rows.append(gain)
    spare = out_ref.shape[0] - videos - gain.shape[0]
    if spare:
        rows.append(jnp.zeros((spare, LANES), F32))
    out_ref[...] = jnp.concatenate(rows, axis=0)


def index_kernel(message_ref, out_ref):
    peer = lax.broadcasted_iota(jnp.int32, (out_ref.shape[0], 1, LANES), 0).astype(F32)
    row = lax.broadcasted_iota(jnp.int32, message_ref.shape, 0)
    lane = lax.broadcasted_iota(jnp.int32, message_ref.shape, 1)
    free = jnp.logical_and(row == 0, lane == KMAX + 1)
    out_ref[...] = jnp.where(free[None], peer, message_ref[...][None])


def select_kernel(index_ref, video_ref, out_ref):
    frames = index_ref.shape[0]
    videos, _, patches, width = video_ref.shape
    seq = frames * TOKL
    half = width // 2
    own = out_ref.shape[1] // 2
    row = lax.broadcasted_iota(jnp.int32, (frames, frames), 0)
    col = lax.broadcasted_iota(jnp.int32, (frames, frames), 1)
    before = (col < row).astype(BF16)
    token = lax.broadcasted_iota(jnp.int32, (frames, seq), 1)
    patch = lax.broadcasted_iota(jnp.int32, (frames, patches), 1).astype(F32)
    for v in range(videos):
        table = index_ref[:, v, :]
        count = table[:, KMAX : KMAX + 1]
        offset = dot32(before, jnp.broadcast_to(count, (frames, LANES)).astype(BF16))[:, :1]
        place = token.astype(F32) - offset
        at_token, at_patch = [], []
        for s in range(KMAX):
            live = jnp.logical_and(place == s, count > s)
            at_token.append(jnp.where(live, 1.0, 0.0))
            at_patch.append(jnp.where(table[:, s : s + 1] == patch, 1.0, 0.0))
        at_token = jnp.concatenate(at_token, axis=0).astype(BF16)
        at_patch = jnp.concatenate(at_patch, axis=0).astype(BF16)
        chosen = lax.dot_general(
            at_token, at_patch, (((0,), (0,)), ((), ())), preferred_element_type=F32
        ).astype(BF16)
        taken = dot32(chosen, video_ref[v, 0]).astype(BF16)
        base = v * seq
        for peer in range(base // own, (base + seq) // own):
            first = peer * own - base
            rows = taken[first : first + own]
            out_ref[peer] = jnp.concatenate([rows[:, :half], rows[:, half:]], axis=0)


def attend_kernel(index_ref, rows_ref, w_qkv_ref, w_out_ref, out_ref):
    frames, packed, half = rows_ref.shape
    own = packed // 2
    width = 2 * half
    heads = width // HEAD_DIM
    seq = frames * TOKL
    videos = frames * own // seq
    raw = rows_ref[...].astype(F32)

    def feature_mean(values):
        part = jnp.sum(values, axis=-1, keepdims=True)
        return (part + swap_halves(part)) / width

    centred = raw - feature_mean(raw)
    variance = feature_mean(centred * centred)
    normed = (centred * lax.rsqrt(variance + NORM_EPS)).astype(BF16).reshape(-1, half)

    def project(start):
        low = dot32(normed, w_qkv_ref[:half, start : start + width])
        high = dot32(normed, w_qkv_ref[half:, start : start + width])
        low = low.reshape(frames, packed, width)
        high = high.reshape(frames, packed, width)
        return (low + swap_halves(high)).astype(BF16).astype(F32)

    table = index_ref[...]
    row = lax.broadcasted_iota(jnp.int32, (1, packed, 1), 1)
    me = table[:1, :1, KMAX + 1 : KMAX + 2].astype(jnp.int32)
    flat = me * own + jnp.where(row >= own, row - own, row)
    owner = jnp.zeros((frames, packed, 1), jnp.bool_)
    for v in range(videos):
        count = table[:, v : v + 1, KMAX : KMAX + 1]
        upto = count
        step = 1
        while step < frames:
            moved = jnp.concatenate([jnp.zeros((step, 1, 1), F32), upto[:-step]], axis=0)
            upto = upto + moved
            step *= 2
        place = (flat - v * seq).astype(F32)
        inside = jnp.logical_and(place >= upto - count, place < upto)
        ours = jnp.logical_and(flat >= v * seq, flat < (v + 1) * seq)
        owner = jnp.logical_or(owner, jnp.logical_and(inside, ours))

    def of_owner(values):
        return jnp.sum(jnp.where(owner, values, 0.0), axis=0)

    query = of_owner(project(0))
    product = (project(width) * query[None]).reshape(-1, width)
    feature = lax.broadcasted_iota(jnp.int32, (width, LANES), 0) // HEAD_DIM
    head = lax.broadcasted_iota(jnp.int32, (width, LANES), 1)
    to_head = jnp.where(feature == head, 1.0, 0.0).astype(BF16)
    coarse = product.astype(BF16)
    rest = product - coarse.astype(F32)
    fine = rest.astype(BF16)
    last = (rest - fine.astype(F32)).astype(BF16)
    scores = dot32(coarse, to_head) + dot32(fine, to_head) + dot32(last, to_head)
    scores = scores.reshape(frames, packed, LANES) * SCORE_SCALE
    raised = jnp.exp(scores - jnp.max(scores, axis=0, keepdims=True))
    weights = (raised / jnp.sum(raised, axis=0, keepdims=True)).astype(BF16)
    head = lax.broadcasted_iota(jnp.int32, (LANES, width), 0)
    feature = lax.broadcasted_iota(jnp.int32, (LANES, width), 1) // HEAD_DIM
    from_head = jnp.where(feature == head, 1.0, 0.0).astype(BF16)
    spread = dot32(weights.reshape(-1, LANES), from_head).reshape(frames, packed, width)
    attended = jnp.sum(spread * project(2 * width), axis=0).astype(BF16)
    change = dot32(attended, w_out_ref[...])
    place = lax.broadcasted_iota(jnp.int32, (packed, half), 0)
    change = jnp.where(place < own, change[:, :half], swap_halves(change[:, half:]))
    encoded = (of_owner(raw) + change).astype(BF16)
    out_ref[...] = jnp.broadcast_to(encoded[None], out_ref.shape)


def project_kernel(rows_ref, w_proj_ref, gain_ref, out_ref):
    frames, packed, half = rows_ref.shape
    own = packed // 2
    tokens = frames * own
    rows = rows_ref[...].reshape(frames * packed, half)
    token = lax.broadcasted_iota(jnp.int32, (tokens, frames * packed), 0)
    source = lax.broadcasted_iota(jnp.int32, (tokens, frames * packed), 1)
    first = (token // own) * packed + token % own
    low = dot32(jnp.where(source == first, 1.0, 0.0).astype(BF16), rows).astype(BF16)
    high = dot32(jnp.where(source == first + own, 1.0, 0.0).astype(BF16), rows).astype(BF16)
    total = dot32(low, w_proj_ref[:half, :]) + dot32(high, w_proj_ref[half:, :])
    gain = gain_ref[...].astype(F32)
    lanes = gain.shape[1]
    for r in range(gain.shape[0]):
        piece = slice(r * lanes, (r + 1) * lanes)
        gained = (total[:, piece] * gain[r : r + 1]).astype(BF16)
        out_ref[:, piece] = gained


def products(place_of, videos, index_ref, rows_ref, w_gate_ref, w_up_ref, begun, emit):
    parts, tokens, columns = rows_ref.shape
    gain_rows = -(-columns // LANES)
    places = [place_of(part) for part in range(parts)]
    squares = jnp.zeros((tokens, LANES), F32) if begun is None else begun[2][...]
    for part, place in enumerate(places):
        inverse = 1.0 / index_ref[place, videos : videos + gain_rows, :]
        for r in range(gain_rows):
            piece = rows_ref[part, :, r * LANES : min((r + 1) * LANES, columns)].astype(F32)
            piece = piece * inverse[r : r + 1, : piece.shape[1]]
            piece = piece * piece
            if piece.shape[1] < LANES:
                fill = jnp.zeros((tokens, LANES - piece.shape[1]), F32)
                piece = jnp.concatenate([piece, fill], axis=1)
            squares = squares + piece
    width = w_gate_ref.shape[1]
    block = min(width, 256)
    for first in range(0, width, block):
        sums = []
        for i, w_ref in enumerate((w_gate_ref, w_up_ref)):
            total = None if begun is None else begun[i][:, first : first + block]
            for part, place in enumerate(places):
                depth = pl.ds(pl.multiple_of(place * columns, columns), columns)
                one = dot32(rows_ref[part], w_ref[depth, first : first + block])
                total = one if total is None else total + one
            sums.append(total)
        emit(first, block, *sums)
    return squares


def place_rule(index_ref, outer, flip):
    me = jnp.max(index_ref[0, :1, KMAX + 1 : KMAX + 2]).astype(jnp.int32)
    quad = index_ref.shape[0] // outer
    row = me // quad
    near = jnp.bitwise_xor(me - row * quad, flip)
    if outer <= DIRECT:
        return lambda i: jnp.bitwise_xor(row, i) * quad + near
    return lambda i: i * quad + near


def partial_kernel(flip, videos, *refs):
    index_ref, rows_ref, w_gate_ref, w_up_ref = refs[:4]
    gate_ref, up_ref, squares_ref = refs[-3:]
    begun = refs[4:7] if len(refs) > 7 else None

    def emit(first, block, gate, up):
        gate_ref[:, first : first + block] = gate
        up_ref[:, first : first + block] = up

    rule = place_rule(index_ref, rows_ref.shape[0], flip)
    squares_ref[...] = products(
        rule, videos, index_ref, rows_ref, w_gate_ref, w_up_ref, begun, emit
    )


def final_kernel(flip, index_ref, rows_ref, w_gate_ref, w_up_ref, gate_ref, up_ref, squares_ref,
                 out_ref, gate_sum, up_sum):
    def emit(first, block, gate, up):
        gate_sum[:, first : first + block] = gate
        up_sum[:, first : first + block] = up

    rule = place_rule(index_ref, rows_ref.shape[0], flip)
    begun = (gate_ref, up_ref, squares_ref)
    squares = products(
        rule, out_ref.shape[0], index_ref, rows_ref, w_gate_ref, w_up_ref, begun, emit
    )
    mean = jnp.sum(squares, axis=1, keepdims=True) / w_gate_ref.shape[0]
    scale = lax.rsqrt(mean + NORM_EPS)
    hidden = jax.nn.silu(gate_sum[...] * scale) * (up_sum[...] * scale)
    out_ref[...] = hidden.astype(BF16).reshape(out_ref.shape)


def local(video, w_qkv, w_out, keep_list, kept_counts, w_proj, llm_gain, w_gate, w_up):
    videos, _, patches, width = video.shape
    axes = ("outer", "mid", "cores")
    frames, outer = lax.axis_size(axes), lax.axis_size("outer")
    seq = frames * TOKL
    tokens = videos * seq
    packed = 2 * (tokens // frames)
    half = width // 2
    columns = w_proj.shape[1]
    spread = functools.partial(lax.all_to_all, split_axis=0, concat_axis=0, tiled=True)
    gain_rows = -(-columns // LANES)
    gain = llm_gain.reshape(gain_rows, -1)

    counts, listed = kept_counts.T, keep_list
    rows = -(-(videos + gain_rows) // 8) * 8
    message = pl.pallas_call(
        collect_kernel,
        out_shape=jax.ShapeDtypeStruct((rows, LANES), F32),
        in_specs=[whole(pltpu.HBM)] * 3,
        out_specs=whole(),
        scratch_shapes=[pltpu.VMEM(x.shape, x.dtype) for x in (counts, listed, gain)]
        + [pltpu.SemaphoreType.DMA((3,))],
        compiler_params=params(2 * MIB),
        name="collect",
    )(*(pltpu.with_memory_space_constraint(x, pltpu.HBM) for x in (counts, listed, gain)))
    message = pl.pallas_call(
        index_kernel,
        out_shape=jax.ShapeDtypeStruct((frames, rows, LANES), F32),
        in_specs=[whole()],
        out_specs=whole(),
        compiler_params=params(2 * MIB),
        cost_estimate=pl.CostEstimate(flops=COVER_FLOPS, bytes_accessed=65536, transcendentals=0),
        name="index",
    )(message)
    index = spread(message, axes)

    chosen = pl.pallas_call(
        select_kernel,
        out_shape=jax.ShapeDtypeStruct((frames, packed, half), BF16),
        in_specs=[whole(), whole()],
        out_specs=whole(),
        compiler_params=params(3 * MIB + 8 * tokens * width),
        name="select",
    )(index, video)
    seen = spread(chosen, axes)

    encoded = pl.pallas_call(
        attend_kernel,
        out_shape=jax.ShapeDtypeStruct((frames, packed, half), BF16),
        in_specs=[whole()] * 4,
        out_specs=whole(),
        compiler_params=params(4 * MIB + 24 * frames * packed * width),
        name="attend",
    )(index, seen, w_qkv, w_out)
    token_rows = spread(encoded, axes)

    gained = pl.pallas_call(
        project_kernel,
        out_shape=jax.ShapeDtypeStruct((tokens, columns), BF16),
        in_specs=[whole(), whole(), whole()],
        out_specs=whole(),
        compiler_params=params(4 * MIB + 16 * tokens * columns),
        name="project",
    )(token_rows, w_proj, gain)

    def swap(values, axis, flip=1):
        pairs = [(i, i ^ flip) for i in range(lax.axis_size(axis))]
        return lax.ppermute(values, axis, pairs)

    if outer <= DIRECT:
        line = jnp.stack([gained] + [swap(gained, "outer", k) for k in range(1, outer)])
    else:
        line = spread(jnp.broadcast_to(gained[None], (outer,) + gained.shape), "outer")
    units = w_gate.shape[1]
    part = jax.ShapeDtypeStruct((tokens, units), F32)
    sums = (part, part, jax.ShapeDtypeStruct((tokens, LANES), F32))
    work = pl.CostEstimate(
        flops=tokens * w_gate.shape[0] * units,
        bytes_accessed=w_gate.shape[0] * units,
        transcendentals=0,
    )

    def add(name, flip, block, begun):
        return pl.pallas_call(
            functools.partial(partial_kernel, flip, videos),
            out_shape=sums,
            in_specs=[whole()] * (4 + len(begun)),
            out_specs=(whole(), whole(), whole()),
            compiler_params=params(3 * MIB + 20 * tokens * units),
            cost_estimate=work,
            name=name,
        )(index, block, w_gate, w_up, *begun)

    line_mid = swap(line, "mid")
    line_core = swap(line, "cores")
    begun = add("own", 0, line, ())
    begun = add("core", 1, line_core, begun)
    line_mid, begun = lax.optimization_barrier((line_mid, begun))
    line_both = swap(line_mid, "cores")
    begun = add("mid", 2, line_mid, begun)
    return pl.pallas_call(
        functools.partial(final_kernel, 3),
        out_shape=jax.ShapeDtypeStruct((videos, seq, units), BF16),
        in_specs=[whole()] * 7,
        out_specs=whole(),
        scratch_shapes=[pltpu.VMEM((tokens, units), F32)] * 2,
        compiler_params=params(3 * MIB + 24 * tokens * units),
        cost_estimate=work,
        name="final",
    )(index, line_both, w_gate, w_up, *begun)


def solution(mesh):
    groups, frames = mesh.devices.shape
    devices = mesh.devices.reshape(groups, frames // 4, 2, 2)
    split = Mesh(devices, ("groups", "outer", "mid", "cores"))
    spread = ("outer", "mid", "cores")
    in_specs = (
        P("groups", spread, None, None),
        P(),
        P(),
        P("groups", spread, None),
        P("groups", spread),
        P(None, spread),
        P(spread),
        P(None, spread),
        P(None, spread),
    )
    out_specs = P("groups", None, spread)
    return jax.shard_map(local, mesh=split, in_specs=in_specs, out_specs=out_specs, check_vma=False)
```

```python
import functools

import jax
import jax.numpy as jnp
from jax import lax
from jax.experimental import pallas as pl
from jax.experimental.pallas import tpu as pltpu
from jax.sharding import Mesh
from jax.sharding import PartitionSpec as P

HEAD_DIM = 64
TOKL = 2
KMAX = 4
LANES = 128
NORM_EPS = 1e-05
SCORE_SCALE = 0.125
DIRECT = 4
NEAR = 4
MIB = 1 << 20
COVER_FLOPS = 20_000_000_000
F32 = jnp.float32
BF16 = jnp.bfloat16


def dot32(left, right):
    return jnp.dot(left, right, preferred_element_type=F32)


def swap_halves(values):
    rows = values.shape[-2] // 2
    return jnp.concatenate([values[..., rows:, :], values[..., :rows, :]], axis=-2)


def whole(space=pltpu.VMEM):
    return pl.BlockSpec(memory_space=space)


def params(limit):
    return pltpu.CompilerParams(vmem_limit_bytes=int(limit))


def collect_kernel(counts_hbm, keep_hbm, gain_hbm, out_ref, counts_ref, keep_ref, gain_ref, sems):
    arrays = ((counts_hbm, counts_ref), (keep_hbm, keep_ref), (gain_hbm, gain_ref))
    copies = [
        pltpu.make_async_copy(source, target, sems.at[i])
        for i, (source, target) in enumerate(arrays)
    ]
    for copy in copies:
        copy.start()
    for copy in copies:
        copy.wait()
    videos = keep_ref.shape[0]
    lane = lax.broadcasted_iota(jnp.int32, (1, LANES), 1)
    counts = counts_ref[...].astype(F32)
    rows = []
    for v in range(videos):
        listed = keep_ref[v, :, :LANES].astype(F32)
        rows.append(jnp.where(lane == KMAX, counts[:, v : v + 1], listed))
    gain = gain_ref[...].astype(F32)
    if gain.shape[1] < LANES:
        fill = jnp.ones((gain.shape[0], LANES - gain.shape[1]), F32)
        gain = jnp.concatenate([gain, fill], axis=1)
    rows.append(gain)
    spare = out_ref.shape[0] - videos - gain.shape[0]
    if spare:
        rows.append(jnp.zeros((spare, LANES), F32))
    out_ref[...] = jnp.concatenate(rows, axis=0)


def index_kernel(message_ref, out_ref):
    peer = lax.broadcasted_iota(jnp.int32, (out_ref.shape[0], 1, LANES), 0).astype(F32)
    row = lax.broadcasted_iota(jnp.int32, message_ref.shape, 0)
    lane = lax.broadcasted_iota(jnp.int32, message_ref.shape, 1)
    free = jnp.logical_and(row == 0, lane == KMAX + 1)
    out_ref[...] = jnp.where(free[None], peer, message_ref[...][None])


def select_kernel(index_ref, video_ref, out_ref):
    frames = index_ref.shape[0]
    videos, _, patches, width = video_ref.shape
    seq = frames * TOKL
    half = width // 2
    own = out_ref.shape[1] // 2
    row = lax.broadcasted_iota(jnp.int32, (frames, frames), 0)
    col = lax.broadcasted_iota(jnp.int32, (frames, frames), 1)
    before = (col < row).astype(BF16)
    token = lax.broadcasted_iota(jnp.int32, (frames, seq), 1)
    patch = lax.broadcasted_iota(jnp.int32, (frames, patches), 1).astype(F32)
    for v in range(videos):
        table = index_ref[:, v, :]
        count = table[:, KMAX : KMAX + 1]
        offset = dot32(before, jnp.broadcast_to(count, (frames, LANES)).astype(BF16))[:, :1]
        place = token.astype(F32) - offset
        at_token, at_patch = [], []
        for s in range(KMAX):
            live = jnp.logical_and(place == s, count > s)
            at_token.append(jnp.where(live, 1.0, 0.0))
            at_patch.append(jnp.where(table[:, s : s + 1] == patch, 1.0, 0.0))
        at_token = jnp.concatenate(at_token, axis=0).astype(BF16)
        at_patch = jnp.concatenate(at_patch, axis=0).astype(BF16)
        chosen = lax.dot_general(
            at_token, at_patch, (((0,), (0,)), ((), ())), preferred_element_type=F32
        ).astype(BF16)
        taken = dot32(chosen, video_ref[v, 0]).astype(BF16)
        base = v * seq
        for peer in range(base // own, (base + seq) // own):
            first = peer * own - base
            rows = taken[first : first + own]
            out_ref[peer] = jnp.concatenate([rows[:, :half], rows[:, half:]], axis=0)


def attend_kernel(index_ref, rows_ref, w_qkv_ref, w_out_ref, out_ref):
    frames, packed, half = rows_ref.shape
    own = packed // 2
    width = 2 * half
    seq = frames * TOKL
    videos = frames * own // seq
    raw = rows_ref[...].astype(F32)

    def feature_mean(values):
        part = jnp.sum(values, axis=-1, keepdims=True)
        return (part + swap_halves(part)) / width

    centred = raw - feature_mean(raw)
    variance = feature_mean(centred * centred)
    normed = (centred * lax.rsqrt(variance + NORM_EPS)).astype(BF16).reshape(-1, half)

    def project(start):
        low = dot32(normed, w_qkv_ref[:half, start : start + width])
        high = dot32(normed, w_qkv_ref[half:, start : start + width])
        low = low.reshape(frames, packed, width)
        high = high.reshape(frames, packed, width)
        return (low + swap_halves(high)).astype(BF16).astype(F32)

    table = index_ref[...]
    row = lax.broadcasted_iota(jnp.int32, (1, packed, 1), 1)
    me = table[:1, :1, KMAX + 1 : KMAX + 2].astype(jnp.int32)
    flat = me * own + jnp.where(row >= own, row - own, row)
    owner = jnp.zeros((frames, packed, 1), jnp.bool_)
    for v in range(videos):
        count = table[:, v : v + 1, KMAX : KMAX + 1]
        upto = count
        step = 1
        while step < frames:
            moved = jnp.concatenate([jnp.zeros((step, 1, 1), F32), upto[:-step]], axis=0)
            upto = upto + moved
            step *= 2
        place = (flat - v * seq).astype(F32)
        inside = jnp.logical_and(place >= upto - count, place < upto)
        ours = jnp.logical_and(flat >= v * seq, flat < (v + 1) * seq)
        owner = jnp.logical_or(owner, jnp.logical_and(inside, ours))

    def of_owner(values):
        return jnp.sum(jnp.where(owner, values, 0.0), axis=0)

    query = of_owner(project(0))
    product = (project(width) * query[None]).reshape(-1, width)
    feature = lax.broadcasted_iota(jnp.int32, (width, LANES), 0) // HEAD_DIM
    head = lax.broadcasted_iota(jnp.int32, (width, LANES), 1)
    to_head = jnp.where(feature == head, 1.0, 0.0).astype(BF16)
    coarse = product.astype(BF16)
    rest = product - coarse.astype(F32)
    fine = rest.astype(BF16)
    last = (rest - fine.astype(F32)).astype(BF16)
    scores = dot32(coarse, to_head) + dot32(fine, to_head) + dot32(last, to_head)
    scores = scores.reshape(frames, packed, LANES) * SCORE_SCALE
    raised = jnp.exp(scores - jnp.max(scores, axis=0, keepdims=True))
    weights = (raised / jnp.sum(raised, axis=0, keepdims=True)).astype(BF16)
    head = lax.broadcasted_iota(jnp.int32, (LANES, width), 0)
    feature = lax.broadcasted_iota(jnp.int32, (LANES, width), 1) // HEAD_DIM
    from_head = jnp.where(feature == head, 1.0, 0.0).astype(BF16)
    spread = dot32(weights.reshape(-1, LANES), from_head).reshape(frames, packed, width)
    attended = jnp.sum(spread * project(2 * width), axis=0).astype(BF16)
    change = dot32(attended, w_out_ref[...])
    place = lax.broadcasted_iota(jnp.int32, (packed, half), 0)
    change = jnp.where(place < own, change[:, :half], swap_halves(change[:, half:]))
    encoded = (of_owner(raw) + change).astype(BF16)
    out_ref[...] = jnp.broadcast_to(encoded[None], out_ref.shape)


def project_kernel(rows_ref, w_proj_ref, gain_ref, out_ref):
    frames, packed, half = rows_ref.shape
    own = packed // 2
    tokens = frames * own
    rows = rows_ref[...].reshape(frames * packed, half)
    token = lax.broadcasted_iota(jnp.int32, (tokens, frames * packed), 0)
    source = lax.broadcasted_iota(jnp.int32, (tokens, frames * packed), 1)
    first = (token // own) * packed + token % own
    low = dot32(jnp.where(source == first, 1.0, 0.0).astype(BF16), rows).astype(BF16)
    high = dot32(jnp.where(source == first + own, 1.0, 0.0).astype(BF16), rows).astype(BF16)
    total = dot32(low, w_proj_ref[:half, :]) + dot32(high, w_proj_ref[half:, :])
    gain = gain_ref[...].astype(F32)
    lanes = gain.shape[1]
    for r in range(gain.shape[0]):
        piece = slice(r * lanes, (r + 1) * lanes)
        gained = (total[:, piece] * gain[r : r + 1]).astype(BF16)
        out_ref[:, piece] = gained


def products(place_of, videos, index_ref, rows_ref, w_gate_ref, w_up_ref, begun, emit):
    parts, tokens, columns = rows_ref.shape
    gain_rows = -(-columns // LANES)
    places = [place_of(part) for part in range(parts)]
    squares = jnp.zeros((tokens, LANES), F32) if begun is None else begun[2][...]
    for part, place in enumerate(places):
        inverse = 1.0 / index_ref[place, videos : videos + gain_rows, :]
        for r in range(gain_rows):
            piece = rows_ref[part, :, r * LANES : min((r + 1) * LANES, columns)].astype(F32)
            piece = piece * inverse[r : r + 1, : piece.shape[1]]
            piece = piece * piece
            if piece.shape[1] < LANES:
                fill = jnp.zeros((tokens, LANES - piece.shape[1]), F32)
                piece = jnp.concatenate([piece, fill], axis=1)
            squares = squares + piece
    width = w_gate_ref.shape[1]
    block = min(width, 256)
    for first in range(0, width, block):
        sums = []
        for i, w_ref in enumerate((w_gate_ref, w_up_ref)):
            total = None if begun is None else begun[i][:, first : first + block]
            for part, place in enumerate(places):
                depth = pl.ds(pl.multiple_of(place * columns, columns), columns)
                one = dot32(rows_ref[part], w_ref[depth, first : first + block])
                total = one if total is None else total + one
            sums.append(total)
        emit(first, block, *sums)
    return squares


def place_rule(index_ref, source):
    flip, steps, direct = source
    me = jnp.max(index_ref[0, :1, KMAX + 1 : KMAX + 2]).astype(jnp.int32)
    row = me // NEAR
    near = jnp.bitwise_xor(me - row * NEAR, flip)
    if direct:
        return lambda i: jnp.bitwise_xor(row, steps[i]) * NEAR + near
    return lambda i: steps[i] * NEAR + near


def partial_kernel(source, videos, *refs):
    index_ref, rows_ref, w_gate_ref, w_up_ref = refs[:4]
    gate_ref, up_ref, squares_ref = refs[-3:]
    begun = refs[4:7] if len(refs) > 7 else None

    def emit(first, block, gate, up):
        gate_ref[:, first : first + block] = gate
        up_ref[:, first : first + block] = up

    rule = place_rule(index_ref, source)
    squares_ref[...] = products(
        rule, videos, index_ref, rows_ref, w_gate_ref, w_up_ref, begun, emit
    )


def final_kernel(source, index_ref, rows_ref, w_gate_ref, w_up_ref, gate_ref, up_ref, squares_ref,
                 out_ref, gate_sum, up_sum):
    def emit(first, block, gate, up):
        gate_sum[:, first : first + block] = gate
        up_sum[:, first : first + block] = up

    rule = place_rule(index_ref, source)
    begun = (gate_ref, up_ref, squares_ref)
    squares = products(
        rule, out_ref.shape[0], index_ref, rows_ref, w_gate_ref, w_up_ref, begun, emit
    )
    mean = jnp.sum(squares, axis=1, keepdims=True) / w_gate_ref.shape[0]
    scale = lax.rsqrt(mean + NORM_EPS)
    hidden = jax.nn.silu(gate_sum[...] * scale) * (up_sum[...] * scale)
    out_ref[...] = hidden.astype(BF16).reshape(out_ref.shape)


def program(video, w_qkv, w_out, keep_list, kept_counts, w_proj, llm_gain, w_gate, w_up):
    videos, _, _, width = video.shape
    axes = ("outer", "mid", "cores")
    frames, outer = lax.axis_size(axes), lax.axis_size("outer")
    seq = frames * TOKL
    tokens = videos * seq
    packed = 2 * (tokens // frames)
    half = width // 2
    columns = w_proj.shape[1]
    spread = functools.partial(lax.all_to_all, split_axis=0, concat_axis=0, tiled=True)
    gain_rows = -(-columns // LANES)
    gain = llm_gain.reshape(gain_rows, -1)

    counts, listed = kept_counts.T, keep_list
    rows = -(-(videos + gain_rows) // 8) * 8
    message = pl.pallas_call(
        collect_kernel,
        out_shape=jax.ShapeDtypeStruct((rows, LANES), F32),
        in_specs=[whole(pltpu.HBM)] * 3,
        out_specs=whole(),
        scratch_shapes=[pltpu.VMEM(x.shape, x.dtype) for x in (counts, listed, gain)]
        + [pltpu.SemaphoreType.DMA((3,))],
        compiler_params=params(2 * MIB),
        name="collect",
    )(*(pltpu.with_memory_space_constraint(x, pltpu.HBM) for x in (counts, listed, gain)))
    message = pl.pallas_call(
        index_kernel,
        out_shape=jax.ShapeDtypeStruct((frames, rows, LANES), F32),
        in_specs=[whole()],
        out_specs=whole(),
        compiler_params=params(2 * MIB),
        cost_estimate=pl.CostEstimate(flops=COVER_FLOPS, bytes_accessed=65536, transcendentals=0),
        name="index",
    )(message)
    index = spread(message, axes)

    chosen = pl.pallas_call(
        select_kernel,
        out_shape=jax.ShapeDtypeStruct((frames, packed, half), BF16),
        in_specs=[whole(), whole()],
        out_specs=whole(),
        compiler_params=params(3 * MIB + 8 * tokens * width),
        name="select",
    )(index, video)
    seen = spread(chosen, axes)

    encoded = pl.pallas_call(
        attend_kernel,
        out_shape=jax.ShapeDtypeStruct((frames, packed, half), BF16),
        in_specs=[whole()] * 4,
        out_specs=whole(),
        compiler_params=params(4 * MIB + 24 * frames * packed * width),
        name="attend",
    )(index, seen, w_qkv, w_out)
    token_rows = spread(encoded, axes)

    gained = pl.pallas_call(
        project_kernel,
        out_shape=jax.ShapeDtypeStruct((tokens, columns), BF16),
        in_specs=[whole(), whole(), whole()],
        out_specs=whole(),
        compiler_params=params(4 * MIB + 16 * tokens * columns),
        name="project",
    )(token_rows, w_proj, gain)

    def swap(values, axis, flip=1):
        pairs = [(i, i ^ flip) for i in range(lax.axis_size(axis))]
        return lax.ppermute(values, axis, pairs)

    units = w_gate.shape[1]
    part = jax.ShapeDtypeStruct((tokens, units), F32)
    sums = (part, part, jax.ShapeDtypeStruct((tokens, LANES), F32))
    work = pl.CostEstimate(
        flops=tokens * w_gate.shape[0] * units // 2,
        bytes_accessed=w_gate.shape[0] * units // 2,
        transcendentals=0,
    )

    def add(source, block, begun):
        return pl.pallas_call(
            functools.partial(partial_kernel, source, videos),
            out_shape=sums,
            in_specs=[whole()] * (4 + len(begun)),
            out_specs=(whole(), whole(), whole()),
            compiler_params=params(3 * MIB + 20 * tokens * units),
            cost_estimate=work,
            name="part",
        )(index, block, w_gate, w_up, *begun)

    direct = outer <= DIRECT
    if direct:
        blocks = [gained] + [swap(gained, "outer", k) for k in range(1, outer)]
        groups = [tuple(range(outer))[i : i + 2] for i in range(0, outer, 2)]
        lines = [jnp.stack([blocks[i] for i in steps]) for steps in groups]
    else:
        groups = [tuple(range(outer))]
        lines = [spread(jnp.broadcast_to(gained[None], (outer,) + gained.shape), "outer")]
    begun = ()
    mids = []
    for steps, line in zip(groups, lines):
        mids.append(swap(line, "mid"))
        line_core = swap(line, "cores")
        begun = add((0, steps, direct), line, begun)
        begun = add((1, steps, direct), line_core, begun)
    for i, steps in enumerate(groups):
        line_core = swap(mids[i], "cores")
        begun = add((2, steps, direct), mids[i], begun)
        if i + 1 < len(groups):
            begun = add((3, steps, direct), line_core, begun)
    return pl.pallas_call(
        functools.partial(final_kernel, (3, groups[-1], direct)),
        out_shape=jax.ShapeDtypeStruct((videos, seq, units), BF16),
        in_specs=[whole()] * 7,
        out_specs=whole(),
        scratch_shapes=[pltpu.VMEM((tokens, units), F32)] * 2,
        compiler_params=params(3 * MIB + 24 * tokens * units),
        cost_estimate=work,
        name="final",
    )(index, line_core, w_gate, w_up, *begun)


def solution(mesh):
    groups, frames = mesh.devices.shape
    devices = mesh.devices.reshape(groups, frames // 4, 2, 2)
    split = Mesh(devices, ("groups", "outer", "mid", "cores"))
    spread = ("outer", "mid", "cores")
    in_specs = (
        P("groups", spread, None, None),
        P(),
        P(),
        P("groups", spread, None),
        P("groups", spread),
        P(None, spread),
        P(spread),
        P(None, spread),
        P(None, spread),
    )
    out_specs = P("groups", None, spread)
    return jax.shard_map(
        program, mesh=split, in_specs=in_specs, out_specs=out_specs, check_vma=False
    )
```

```python
import functools

import jax
import jax.numpy as jnp
from jax import lax
from jax.experimental import pallas as pl
from jax.experimental.pallas import tpu as pltpu
from jax.sharding import Mesh
from jax.sharding import PartitionSpec as P

HEAD_DIM = 64
TOKL = 2
KMAX = 4
LANES = 128
NORM_EPS = 1e-05
SCORE_SCALE = 0.125
DIRECT = 4
NEAR = 4
MIB = 1 << 20
COVER_FLOPS = 20_000_000_000
F32 = jnp.float32
BF16 = jnp.bfloat16


def dot32(left, right):
    return jnp.dot(left, right, preferred_element_type=F32)


def swap_halves(values):
    rows = values.shape[-2] // 2
    return jnp.concatenate([values[..., rows:, :], values[..., :rows, :]], axis=-2)


def whole(space=pltpu.VMEM):
    return pl.BlockSpec(memory_space=space)


def params(limit):
    return pltpu.CompilerParams(vmem_limit_bytes=int(limit))


def collect_kernel(counts_hbm, keep_hbm, gain_hbm, out_ref, counts_ref, keep_ref, gain_ref, sems):
    arrays = ((counts_hbm, counts_ref), (keep_hbm, keep_ref), (gain_hbm, gain_ref))
    copies = [
        pltpu.make_async_copy(source, target, sems.at[i])
        for i, (source, target) in enumerate(arrays)
    ]
    for copy in copies:
        copy.start()
    for copy in copies:
        copy.wait()
    videos = keep_ref.shape[0]
    lane = lax.broadcasted_iota(jnp.int32, (1, LANES), 1)
    counts = counts_ref[...].astype(F32)
    rows = []
    for v in range(videos):
        listed = keep_ref[v, :, :LANES].astype(F32)
        rows.append(jnp.where(lane == KMAX, counts[:, v : v + 1], listed))
    gain = gain_ref[...].astype(F32)
    if gain.shape[1] < LANES:
        fill = jnp.ones((gain.shape[0], LANES - gain.shape[1]), F32)
        gain = jnp.concatenate([gain, fill], axis=1)
    rows.append(gain)
    spare = out_ref.shape[0] - videos - gain.shape[0]
    if spare:
        rows.append(jnp.zeros((spare, LANES), F32))
    out_ref[...] = jnp.concatenate(rows, axis=0)


def index_kernel(message_ref, out_ref):
    peer = lax.broadcasted_iota(jnp.int32, (out_ref.shape[0], 1, LANES), 0).astype(F32)
    row = lax.broadcasted_iota(jnp.int32, message_ref.shape, 0)
    lane = lax.broadcasted_iota(jnp.int32, message_ref.shape, 1)
    free = jnp.logical_and(row == 0, lane == KMAX + 1)
    out_ref[...] = jnp.where(free[None], peer, message_ref[...][None])


def select_kernel(index_ref, video_ref, out_ref):
    frames = index_ref.shape[0]
    videos, _, patches, width = video_ref.shape
    seq = frames * TOKL
    half = width // 2
    own = out_ref.shape[1] // 2
    row = lax.broadcasted_iota(jnp.int32, (frames, frames), 0)
    col = lax.broadcasted_iota(jnp.int32, (frames, frames), 1)
    before = (col < row).astype(BF16)
    token = lax.broadcasted_iota(jnp.int32, (frames, seq), 1)
    patch = lax.broadcasted_iota(jnp.int32, (frames, patches), 1).astype(F32)
    for v in range(videos):
        table = index_ref[:, v, :]
        count = table[:, KMAX : KMAX + 1]
        offset = dot32(before, jnp.broadcast_to(count, (frames, LANES)).astype(BF16))[:, :1]
        place = token.astype(F32) - offset
        at_token, at_patch = [], []
        for s in range(KMAX):
            live = jnp.logical_and(place == s, count > s)
            at_token.append(jnp.where(live, 1.0, 0.0))
            at_patch.append(jnp.where(table[:, s : s + 1] == patch, 1.0, 0.0))
        at_token = jnp.concatenate(at_token, axis=0).astype(BF16)
        at_patch = jnp.concatenate(at_patch, axis=0).astype(BF16)
        chosen = lax.dot_general(
            at_token, at_patch, (((0,), (0,)), ((), ())), preferred_element_type=F32
        ).astype(BF16)
        taken = dot32(chosen, video_ref[v, 0]).astype(BF16)
        base = v * seq
        for peer in range(base // own, (base + seq) // own):
            first = peer * own - base
            rows = taken[first : first + own]
            out_ref[peer] = jnp.concatenate([rows[:, :half], rows[:, half:]], axis=0)


def unpack(rows, own):
    packs = rows.shape[0] // (2 * own)
    token = lax.broadcasted_iota(jnp.int32, (packs * own, rows.shape[0]), 0)
    source = lax.broadcasted_iota(jnp.int32, (packs * own, rows.shape[0]), 1)
    first = (token // own) * (2 * own) + token % own
    low = dot32(jnp.where(source == first, 1.0, 0.0).astype(BF16), rows)
    high = dot32(jnp.where(source == first + own, 1.0, 0.0).astype(BF16), rows)
    return low, high


def attend_kernel(index_ref, rows_ref, w_qkv_ref, w_out_ref, out_ref):
    frames, packed, half = rows_ref.shape
    own = packed // 2
    width = 2 * half
    seq = frames * TOKL
    videos = frames * own // seq
    low, high = unpack(rows_ref[...].reshape(frames * packed, half), own)
    raw = jnp.concatenate([low, high], axis=1)
    centred = raw - jnp.mean(raw, axis=1, keepdims=True)
    variance = jnp.mean(centred * centred, axis=1, keepdims=True)
    normed = (centred * lax.rsqrt(variance + NORM_EPS)).astype(BF16)

    pairs = frames * own // packed

    def project(start):
        part = dot32(normed, w_qkv_ref[:, start : start + width])
        return part.astype(BF16).astype(F32).reshape(pairs, packed, width)

    table = index_ref[...]
    row = lax.broadcasted_iota(jnp.int32, (1, packed, LANES), 1)
    upper = row >= own
    me = table[:1, :1, KMAX + 1 : KMAX + 2].astype(jnp.int32)
    flat = me * own + jnp.where(upper, row - own, row)
    owner = jnp.zeros((pairs, packed, LANES), F32)
    for v in range(videos):
        count = table[:, v : v + 1, KMAX : KMAX + 1]
        upto = count
        step = 1
        while step < frames:
            moved = jnp.concatenate([jnp.zeros((step, 1, 1), F32), upto[:-step]], axis=0)
            upto = upto + moved
            step *= 2
        place = (flat - v * seq).astype(F32)
        ours = jnp.logical_and(flat >= v * seq, flat < (v + 1) * seq)
        below = upto - count
        below = below.reshape(pairs, 2, 1, 1)
        upto = upto.reshape(pairs, 2, 1, 1)
        start = jnp.where(upper, below[:, 1], below[:, 0])
        stop = jnp.where(upper, upto[:, 1], upto[:, 0])
        inside = jnp.logical_and(place >= start, place < stop)
        owner = owner + jnp.where(jnp.logical_and(inside, ours), 1.0, 0.0)
    owner = owner[:, :, :1]

    def over_frames(values):
        total = jnp.sum(values, axis=0)
        return total + swap_halves(total)

    query = over_frames(project(0) * owner)
    product = (project(width) * query[None]).reshape(-1, width)
    feature = lax.broadcasted_iota(jnp.int32, (width, LANES), 0) // HEAD_DIM
    head = lax.broadcasted_iota(jnp.int32, (width, LANES), 1)
    to_head = jnp.where(feature == head, 1.0, 0.0).astype(BF16)
    coarse = product.astype(BF16)
    rest = product - coarse.astype(F32)
    fine = rest.astype(BF16)
    last = (rest - fine.astype(F32)).astype(BF16)
    scores = dot32(coarse, to_head) + dot32(fine, to_head) + dot32(last, to_head)
    scores = scores.reshape(pairs, packed, LANES) * SCORE_SCALE
    largest = jnp.max(scores, axis=0)
    largest = jnp.maximum(largest, swap_halves(largest))
    raised = jnp.exp(scores - largest[None])
    weights = (raised / over_frames(raised)[None]).astype(BF16)
    head = lax.broadcasted_iota(jnp.int32, (LANES, width), 0)
    feature = lax.broadcasted_iota(jnp.int32, (LANES, width), 1) // HEAD_DIM
    from_head = jnp.where(feature == head, 1.0, 0.0).astype(BF16)
    spread = dot32(weights.reshape(-1, LANES), from_head).reshape(pairs, packed, width)
    attended = over_frames(spread * project(2 * width)).astype(BF16)
    change = dot32(attended, w_out_ref[...])
    residual = over_frames(raw.reshape(pairs, packed, width) * owner)
    encoded = residual + change
    place = lax.broadcasted_iota(jnp.int32, (packed, half), 0)
    encoded = jnp.where(place < own, encoded[:, :half], encoded[:, half:]).astype(BF16)
    out_ref[...] = jnp.broadcast_to(encoded[None], out_ref.shape)


def project_kernel(rows_ref, w_proj_ref, gain_ref, out_ref):
    frames, packed, half = rows_ref.shape
    own = packed // 2
    rows = rows_ref[...].reshape(frames * packed, half)
    low, high = (part.astype(BF16) for part in unpack(rows, own))
    total = dot32(low, w_proj_ref[:half, :]) + dot32(high, w_proj_ref[half:, :])
    gain = gain_ref[...].astype(F32)
    lanes = gain.shape[1]
    for r in range(gain.shape[0]):
        piece = slice(r * lanes, (r + 1) * lanes)
        gained = (total[:, piece] * gain[r : r + 1]).astype(BF16)
        out_ref[:, piece] = gained


def places(index_ref, sources):
    me = jnp.max(index_ref[0, :1, KMAX + 1 : KMAX + 2]).astype(jnp.int32)
    row = me // NEAR
    found = []
    for flip, steps, direct in sources:
        near = jnp.bitwise_xor(me - row * NEAR, flip)
        for i, step in enumerate(steps):
            outer = jnp.bitwise_xor(row, step) if direct else step
            found.append((i, outer * NEAR + near))
    return found


def square_sums(blocks, videos, index_ref):
    tokens, columns = blocks[0][0].shape[1:]
    gain_rows = -(-columns // LANES)
    squares = jnp.zeros((tokens, LANES), F32)
    for rows_ref, i, place in blocks:
        inverse = 1.0 / index_ref[place, videos : videos + gain_rows, :]
        for r in range(gain_rows):
            piece = rows_ref[i, :, r * LANES : min((r + 1) * LANES, columns)].astype(F32)
            piece = piece * inverse[r : r + 1, : piece.shape[1]]
            piece = piece * piece
            if piece.shape[1] < LANES:
                fill = jnp.zeros((tokens, LANES - piece.shape[1]), F32)
                piece = jnp.concatenate([piece, fill], axis=1)
            squares = squares + piece
    return squares


def products(blocks, w_gate_ref, w_up_ref, begun, emit):
    columns = blocks[0][0].shape[2]
    width = w_gate_ref.shape[1]
    block = min(width, 256)
    for first in range(0, width, block):
        sums = []
        for i, w_ref in enumerate((w_gate_ref, w_up_ref)):
            total = begun[i][:, first : first + block] if begun else None
            for rows_ref, part, place in blocks:
                depth = pl.ds(pl.multiple_of(place * columns, columns), columns)
                one = dot32(rows_ref[part], w_ref[depth, first : first + block])
                total = one if total is None else total + one
            sums.append(total)
        emit(first, block, *sums)


def split_refs(sources, refs):
    index_ref, w_gate_ref, w_up_ref = refs[:3]
    rows = refs[3 : 3 + len(sources)]
    owners = [ref for ref, source in zip(rows, sources) for _ in source[1]]
    blocks = [(ref,) + found for ref, found in zip(owners, places(index_ref, sources))]
    return index_ref, w_gate_ref, w_up_ref, blocks, refs[3 + len(sources) :]


def partial_kernel(sources, videos, *refs):
    index_ref, w_gate_ref, w_up_ref, blocks, rest = split_refs(sources, refs)
    begun, (gate_ref, up_ref, squares_ref) = rest[:-3], rest[-3:]

    def emit(first, block, gate, up):
        gate_ref[:, first : first + block] = gate
        up_ref[:, first : first + block] = up

    squares = square_sums(blocks, videos, index_ref)
    squares_ref[...] = squares + begun[2][...] if begun else squares
    products(blocks, w_gate_ref, w_up_ref, begun, emit)


def final_kernel(sources, *refs):
    index_ref, w_gate_ref, w_up_ref, blocks, rest = split_refs(sources, refs)
    begun, out_ref = rest[:3], rest[3]
    videos = out_ref.shape[0]
    squares = begun[2][...] + square_sums(blocks, videos, index_ref)
    mean = jnp.sum(squares, axis=1, keepdims=True) / w_gate_ref.shape[0]
    scale = lax.rsqrt(mean + NORM_EPS)

    def emit(first, block, gate, up):
        hidden = (jax.nn.silu(gate * scale) * (up * scale)).astype(BF16)
        out_ref[:, :, first : first + block] = hidden.reshape(videos, -1, block)

    products(blocks, w_gate_ref, w_up_ref, begun, emit)


def program(video, w_qkv, w_out, keep_list, kept_counts, w_proj, llm_gain, w_gate, w_up):
    videos, _, _, width = video.shape
    axes = ("outer", "mid", "cores")
    frames, outer = lax.axis_size(axes), lax.axis_size("outer")
    seq = frames * TOKL
    tokens = videos * seq
    packed = 2 * (tokens // frames)
    half = width // 2
    columns = w_proj.shape[1]
    spread = functools.partial(lax.all_to_all, split_axis=0, concat_axis=0, tiled=True)
    gain_rows = -(-columns // LANES)
    gain = llm_gain.reshape(gain_rows, -1)

    counts, listed = kept_counts.T, keep_list
    rows = -(-(videos + gain_rows) // 8) * 8
    message = pl.pallas_call(
        collect_kernel,
        out_shape=jax.ShapeDtypeStruct((rows, LANES), F32),
        in_specs=[whole(pltpu.HBM)] * 3,
        out_specs=whole(),
        scratch_shapes=[pltpu.VMEM(x.shape, x.dtype) for x in (counts, listed, gain)]
        + [pltpu.SemaphoreType.DMA((3,))],
        compiler_params=params(2 * MIB),
        name="collect",
    )(*(pltpu.with_memory_space_constraint(x, pltpu.HBM) for x in (counts, listed, gain)))
    message = pl.pallas_call(
        index_kernel,
        out_shape=jax.ShapeDtypeStruct((frames, rows, LANES), F32),
        in_specs=[whole()],
        out_specs=whole(),
        compiler_params=params(2 * MIB),
        cost_estimate=pl.CostEstimate(flops=COVER_FLOPS, bytes_accessed=65536, transcendentals=0),
        name="index",
    )(message)
    index = spread(message, axes)

    chosen = pl.pallas_call(
        select_kernel,
        out_shape=jax.ShapeDtypeStruct((frames, packed, half), BF16),
        in_specs=[whole(), whole()],
        out_specs=whole(),
        compiler_params=params(3 * MIB + 8 * tokens * width),
        name="select",
    )(index, video)
    seen = spread(chosen, axes)

    encoded = pl.pallas_call(
        attend_kernel,
        out_shape=jax.ShapeDtypeStruct((frames, packed, half), BF16),
        in_specs=[whole()] * 4,
        out_specs=whole(),
        compiler_params=params(4 * MIB + 24 * frames * packed * width),
        name="attend",
    )(index, seen, w_qkv, w_out)
    token_rows = spread(encoded, axes)

    gained = pl.pallas_call(
        project_kernel,
        out_shape=jax.ShapeDtypeStruct((tokens, columns), BF16),
        in_specs=[whole(), whole(), whole()],
        out_specs=whole(),
        compiler_params=params(4 * MIB + 16 * tokens * columns),
        name="project",
    )(token_rows, w_proj, gain)

    def swap(values, axis, flip=1):
        pairs = [(i, i ^ flip) for i in range(lax.axis_size(axis))]
        return lax.ppermute(values, axis, pairs)

    units = w_gate.shape[1]
    part = jax.ShapeDtypeStruct((tokens, units), F32)
    sums = (part, part, jax.ShapeDtypeStruct((tokens, LANES), F32))
    work = pl.CostEstimate(
        flops=tokens * w_gate.shape[0] * units // 2,
        bytes_accessed=w_gate.shape[0] * units // 2,
        transcendentals=0,
    )

    direct = outer == DIRECT
    if direct:
        far = [swap(gained, "outer", k) for k in range(1, outer)]
        own = gained[None]
        near, rest = jnp.stack([gained, far[0]]), jnp.stack(far[1:])
        mid0, mid1 = swap(near, "mid"), swap(rest, "mid")
        core = swap(own, "cores")
        core0, core1 = swap(far[0][None], "cores"), swap(rest, "cores")
        both0, both1 = swap(mid0, "cores"), swap(mid1, "cores")
        stages = (
            ((own, 0, (0,)),),
            ((core, 1, (0,)), (far[0][None], 0, (1,))),
            ((core0, 1, (1,)), (rest, 0, (2, 3))),
            ((core1, 1, (2, 3)),),
            ((mid0, 2, (0, 1)),),
            ((both0, 3, (0, 1)),),
            ((mid1, 2, (2, 3)),),
            ((both1, 3, (2, 3)),),
        )
    else:
        line = spread(jnp.broadcast_to(gained[None], (outer,) + gained.shape), "outer")
        steps = tuple(range(outer))
        mid = swap(line, "mid")
        core, both = swap(line, "cores"), swap(mid, "cores")
        blocks = ((line, 0), (core, 1), (mid, 2), (both, 3))
        stages = tuple(((block, flip, steps),) for block, flip in blocks)
    begun = ()
    for i, stage in enumerate(stages):
        sources = tuple((flip, steps, direct) for _, flip, steps in stage)
        last = i + 1 == len(stages)
        begun = pl.pallas_call(
            functools.partial(final_kernel, sources)
            if last
            else functools.partial(partial_kernel, sources, videos),
            out_shape=jax.ShapeDtypeStruct((videos, seq, units), BF16) if last else sums,
            in_specs=[whole()] * (3 + len(stage) + len(begun)),
            out_specs=whole() if last else (whole(),) * 3,
            compiler_params=params(3 * MIB + 20 * tokens * units),
            cost_estimate=work,
            name="final" if last else "part",
        )(index, w_gate, w_up, *(block for block, _, _ in stage), *begun)
    return begun


def solution(mesh):
    groups, frames = mesh.devices.shape
    devices = mesh.devices.reshape(groups, frames // 4, 2, 2)
    split = Mesh(devices, ("groups", "outer", "mid", "cores"))
    spread = ("outer", "mid", "cores")
    in_specs = (
        P("groups", spread, None, None),
        P(),
        P(),
        P("groups", spread, None),
        P("groups", spread),
        P(None, spread),
        P(spread),
        P(None, spread),
        P(None, spread),
    )
    out_specs = P("groups", None, spread)
    return jax.shard_map(
        program, mesh=split, in_specs=in_specs, out_specs=out_specs, check_vma=False
    )
```

```python
import functools

import jax
import jax.numpy as jnp
from jax import lax
from jax.experimental import pallas as pl
from jax.experimental.pallas import tpu as pltpu
from jax.sharding import Mesh
from jax.sharding import PartitionSpec as P

HEAD_DIM = 64
TOKL = 2
KMAX = 4
LANES = 128
NORM_EPS = 1e-05
SCORE_SCALE = 0.125
DIRECT = 4
NEAR = 4
MIB = 1 << 20
COVER_FLOPS = 20_000_000_000
F32 = jnp.float32
BF16 = jnp.bfloat16


def dot32(left, right):
    return jnp.dot(left, right, preferred_element_type=F32)


def swap_halves(values):
    rows = values.shape[-2] // 2
    return jnp.concatenate([values[..., rows:, :], values[..., :rows, :]], axis=-2)


def whole(space=pltpu.VMEM):
    return pl.BlockSpec(memory_space=space)


def params(limit):
    return pltpu.CompilerParams(vmem_limit_bytes=int(limit))


def collect_kernel(counts_hbm, keep_hbm, gain_hbm, out_ref, counts_ref, keep_ref, gain_ref, sems):
    arrays = ((counts_hbm, counts_ref), (keep_hbm, keep_ref), (gain_hbm, gain_ref))
    copies = [
        pltpu.make_async_copy(source, target, sems.at[i])
        for i, (source, target) in enumerate(arrays)
    ]
    for copy in copies:
        copy.start()
    for copy in copies:
        copy.wait()
    videos = keep_ref.shape[0]
    lane = lax.broadcasted_iota(jnp.int32, (1, LANES), 1)
    counts = counts_ref[...].astype(F32)
    rows = []
    for v in range(videos):
        listed = keep_ref[v, :, :LANES].astype(F32)
        rows.append(jnp.where(lane == KMAX, counts[:, v : v + 1], listed))
    gain = gain_ref[...].astype(F32)
    if gain.shape[1] < LANES:
        fill = jnp.ones((gain.shape[0], LANES - gain.shape[1]), F32)
        gain = jnp.concatenate([gain, fill], axis=1)
    rows.append(gain)
    spare = out_ref.shape[0] - videos - gain.shape[0]
    if spare:
        rows.append(jnp.zeros((spare, LANES), F32))
    out_ref[...] = jnp.concatenate(rows, axis=0)


def index_kernel(message_ref, out_ref):
    peer = lax.broadcasted_iota(jnp.int32, (out_ref.shape[0], 1, LANES), 0).astype(F32)
    row = lax.broadcasted_iota(jnp.int32, message_ref.shape, 0)
    lane = lax.broadcasted_iota(jnp.int32, message_ref.shape, 1)
    free = jnp.logical_and(row == 0, lane == KMAX + 1)
    out_ref[...] = jnp.where(free[None], peer, message_ref[...][None])


def select_kernel(index_ref, video_ref, out_ref):
    frames = index_ref.shape[0]
    videos, _, patches, width = video_ref.shape
    seq = frames * TOKL
    half = width // 2
    own = out_ref.shape[1] // 2
    row = lax.broadcasted_iota(jnp.int32, (frames, frames), 0)
    col = lax.broadcasted_iota(jnp.int32, (frames, frames), 1)
    before = (col < row).astype(BF16)
    token = lax.broadcasted_iota(jnp.int32, (frames, seq), 1)
    patch = lax.broadcasted_iota(jnp.int32, (frames, patches), 1).astype(F32)
    for v in range(videos):
        table = index_ref[:, v, :]
        count = table[:, KMAX : KMAX + 1]
        offset = dot32(before, jnp.broadcast_to(count, (frames, LANES)).astype(BF16))[:, :1]
        place = token.astype(F32) - offset
        at_token, at_patch = [], []
        for s in range(KMAX):
            live = jnp.logical_and(place == s, count > s)
            at_token.append(jnp.where(live, 1.0, 0.0))
            at_patch.append(jnp.where(table[:, s : s + 1] == patch, 1.0, 0.0))
        at_token = jnp.concatenate(at_token, axis=0).astype(BF16)
        at_patch = jnp.concatenate(at_patch, axis=0).astype(BF16)
        chosen = lax.dot_general(
            at_token, at_patch, (((0,), (0,)), ((), ())), preferred_element_type=F32
        ).astype(BF16)
        taken = dot32(chosen, video_ref[v, 0]).astype(BF16)
        base = v * seq
        for peer in range(base // own, (base + seq) // own):
            first = peer * own - base
            rows = taken[first : first + own]
            out_ref[peer] = jnp.concatenate([rows[:, :half], rows[:, half:]], axis=0)


def unpack(rows, own):
    packs = rows.shape[0] // (2 * own)
    token = lax.broadcasted_iota(jnp.int32, (packs * own, rows.shape[0]), 0)
    source = lax.broadcasted_iota(jnp.int32, (packs * own, rows.shape[0]), 1)
    first = (token // own) * (2 * own) + token % own
    low = dot32(jnp.where(source == first, 1.0, 0.0).astype(BF16), rows)
    high = dot32(jnp.where(source == first + own, 1.0, 0.0).astype(BF16), rows)
    return low, high


def attend_kernel(index_ref, rows_ref, w_qkv_ref, w_out_ref, out_ref):
    frames, packed, half = rows_ref.shape
    own = packed // 2
    width = 2 * half
    seq = frames * TOKL
    videos = frames * own // seq
    low, high = unpack(rows_ref[...].reshape(frames * packed, half), own)
    raw = jnp.concatenate([low, high], axis=1)
    centred = raw - jnp.mean(raw, axis=1, keepdims=True)
    variance = jnp.mean(centred * centred, axis=1, keepdims=True)
    normed = (centred * lax.rsqrt(variance + NORM_EPS)).astype(BF16)

    pairs = frames * own // packed

    def project(start):
        part = dot32(normed, w_qkv_ref[:, start : start + width])
        return part.astype(BF16).astype(F32).reshape(pairs, packed, width)

    table = index_ref[...]
    row = lax.broadcasted_iota(jnp.int32, (1, packed, LANES), 1)
    upper = row >= own
    me = table[:1, :1, KMAX + 1 : KMAX + 2].astype(jnp.int32)
    flat = me * own + jnp.where(upper, row - own, row)
    owner = jnp.zeros((pairs, packed, LANES), F32)
    for v in range(videos):
        count = table[:, v : v + 1, KMAX : KMAX + 1]
        upto = count
        step = 1
        while step < frames:
            moved = jnp.concatenate([jnp.zeros((step, 1, 1), F32), upto[:-step]], axis=0)
            upto = upto + moved
            step *= 2
        place = (flat - v * seq).astype(F32)
        ours = jnp.logical_and(flat >= v * seq, flat < (v + 1) * seq)
        below = upto - count
        below = below.reshape(pairs, 2, 1, 1)
        upto = upto.reshape(pairs, 2, 1, 1)
        start = jnp.where(upper, below[:, 1], below[:, 0])
        stop = jnp.where(upper, upto[:, 1], upto[:, 0])
        inside = jnp.logical_and(place >= start, place < stop)
        owner = owner + jnp.where(jnp.logical_and(inside, ours), 1.0, 0.0)
    owner = owner[:, :, :1]

    def over_frames(values):
        total = jnp.sum(values, axis=0)
        return total + swap_halves(total)

    query = over_frames(project(0) * owner)
    product = (project(width) * query[None]).reshape(-1, width)
    feature = lax.broadcasted_iota(jnp.int32, (width, LANES), 0) // HEAD_DIM
    head = lax.broadcasted_iota(jnp.int32, (width, LANES), 1)
    to_head = jnp.where(feature == head, 1.0, 0.0).astype(BF16)
    coarse = product.astype(BF16)
    rest = product - coarse.astype(F32)
    fine = rest.astype(BF16)
    last = (rest - fine.astype(F32)).astype(BF16)
    scores = dot32(jnp.concatenate([coarse, fine, last], axis=0), to_head)
    scores = jnp.sum(scores.reshape(3, pairs, packed, LANES), axis=0) * SCORE_SCALE
    largest = jnp.max(scores, axis=0)
    largest = jnp.maximum(largest, swap_halves(largest))
    raised = jnp.exp(scores - largest[None])
    weights = (raised / over_frames(raised)[None]).astype(BF16)
    head = lax.broadcasted_iota(jnp.int32, (LANES, width), 0)
    feature = lax.broadcasted_iota(jnp.int32, (LANES, width), 1) // HEAD_DIM
    from_head = jnp.where(feature == head, 1.0, 0.0).astype(BF16)
    spread = dot32(weights.reshape(-1, LANES), from_head).reshape(pairs, packed, width)
    attended = over_frames(spread * project(2 * width)).astype(BF16)
    change = dot32(attended, w_out_ref[...])
    residual = over_frames(raw.reshape(pairs, packed, width) * owner)
    encoded = residual + change
    place = lax.broadcasted_iota(jnp.int32, (packed, half), 0)
    encoded = jnp.where(place < own, encoded[:, :half], encoded[:, half:]).astype(BF16)
    out_ref[...] = jnp.broadcast_to(encoded[None], out_ref.shape)


def project_kernel(rows_ref, w_proj_ref, gain_ref, out_ref):
    frames, packed, half = rows_ref.shape
    own = packed // 2
    rows = rows_ref[...].reshape(frames * packed, half)
    low, high = (part.astype(BF16) for part in unpack(rows, own))
    total = dot32(low, w_proj_ref[:half, :]) + dot32(high, w_proj_ref[half:, :])
    gain = gain_ref[...].astype(F32)
    lanes = gain.shape[1]
    for r in range(gain.shape[0]):
        piece = slice(r * lanes, (r + 1) * lanes)
        gained = (total[:, piece] * gain[r : r + 1]).astype(BF16)
        out_ref[:, piece] = gained


def places(index_ref, sources):
    me = jnp.max(index_ref[0, :1, KMAX + 1 : KMAX + 2]).astype(jnp.int32)
    row = me // NEAR
    found = []
    for flip, steps, direct in sources:
        near = jnp.bitwise_xor(me - row * NEAR, flip)
        for i, step in enumerate(steps):
            outer = jnp.bitwise_xor(row, step) if direct else step
            found.append((i, outer * NEAR + near))
    return found


def square_sums(blocks, videos, index_ref):
    tokens, columns = blocks[0][0].shape[1:]
    gain_rows = -(-columns // LANES)
    squares = jnp.zeros((tokens, LANES), F32)
    for rows_ref, i, place in blocks:
        inverse = 1.0 / index_ref[place, videos : videos + gain_rows, :]
        for r in range(gain_rows):
            piece = rows_ref[i, :, r * LANES : min((r + 1) * LANES, columns)].astype(F32)
            piece = piece * inverse[r : r + 1, : piece.shape[1]]
            piece = piece * piece
            if piece.shape[1] < LANES:
                fill = jnp.zeros((tokens, LANES - piece.shape[1]), F32)
                piece = jnp.concatenate([piece, fill], axis=1)
            squares = squares + piece
    return squares


def products(blocks, w_gate_ref, w_up_ref, begun, emit):
    columns = blocks[0][0].shape[2]
    width = w_gate_ref.shape[1]
    block = min(width, 256)
    for first in range(0, width, block):
        sums = []
        for i, w_ref in enumerate((w_gate_ref, w_up_ref)):
            total = begun[i][:, first : first + block] if begun else None
            for rows_ref, part, place in blocks:
                depth = pl.ds(pl.multiple_of(place * columns, columns), columns)
                one = dot32(rows_ref[part], w_ref[depth, first : first + block])
                total = one if total is None else total + one
            sums.append(total)
        emit(first, block, *sums)


def split_refs(sources, refs):
    index_ref, w_gate_ref, w_up_ref = refs[:3]
    rows = refs[3 : 3 + len(sources)]
    owners = [ref for ref, source in zip(rows, sources) for _ in source[1]]
    blocks = [(ref,) + found for ref, found in zip(owners, places(index_ref, sources))]
    return index_ref, w_gate_ref, w_up_ref, blocks, refs[3 + len(sources) :]


def partial_kernel(sources, videos, *refs):
    index_ref, w_gate_ref, w_up_ref, blocks, rest = split_refs(sources, refs)
    begun, (gate_ref, up_ref, squares_ref) = rest[:-3], rest[-3:]

    def emit(first, block, gate, up):
        gate_ref[:, first : first + block] = gate
        up_ref[:, first : first + block] = up

    squares = square_sums(blocks, videos, index_ref)
    squares_ref[...] = squares + begun[2][...] if begun else squares
    products(blocks, w_gate_ref, w_up_ref, begun, emit)


def final_kernel(sources, *refs):
    index_ref, w_gate_ref, w_up_ref, blocks, rest = split_refs(sources, refs)
    begun, out_ref = rest[:3], rest[3]
    videos = out_ref.shape[0]
    squares = begun[2][...] + square_sums(blocks, videos, index_ref)
    mean = jnp.sum(squares, axis=1, keepdims=True) / w_gate_ref.shape[0]
    scale = lax.rsqrt(mean + NORM_EPS)

    def emit(first, block, gate, up):
        hidden = (jax.nn.silu(gate * scale) * (up * scale)).astype(BF16)
        out_ref[:, :, first : first + block] = hidden.reshape(videos, -1, block)

    products(blocks, w_gate_ref, w_up_ref, begun, emit)


def program(video, w_qkv, w_out, keep_list, kept_counts, w_proj, llm_gain, w_gate, w_up):
    videos, _, _, width = video.shape
    axes = ("outer", "mid", "cores")
    frames, outer = lax.axis_size(axes), lax.axis_size("outer")
    seq = frames * TOKL
    tokens = videos * seq
    packed = 2 * (tokens // frames)
    half = width // 2
    columns = w_proj.shape[1]
    spread = functools.partial(lax.all_to_all, split_axis=0, concat_axis=0, tiled=True)
    gain_rows = -(-columns // LANES)
    gain = llm_gain.reshape(gain_rows, -1)

    counts, listed = kept_counts.T, keep_list
    rows = -(-(videos + gain_rows) // 8) * 8
    message = pl.pallas_call(
        collect_kernel,
        out_shape=jax.ShapeDtypeStruct((rows, LANES), F32),
        in_specs=[whole(pltpu.HBM)] * 3,
        out_specs=whole(),
        scratch_shapes=[pltpu.VMEM(x.shape, x.dtype) for x in (counts, listed, gain)]
        + [pltpu.SemaphoreType.DMA((3,))],
        compiler_params=params(2 * MIB),
        name="collect",
    )(*(pltpu.with_memory_space_constraint(x, pltpu.HBM) for x in (counts, listed, gain)))
    message = pl.pallas_call(
        index_kernel,
        out_shape=jax.ShapeDtypeStruct((frames, rows, LANES), F32),
        in_specs=[whole()],
        out_specs=whole(),
        compiler_params=params(2 * MIB),
        cost_estimate=pl.CostEstimate(flops=COVER_FLOPS, bytes_accessed=65536, transcendentals=0),
        name="index",
    )(message)
    index = spread(message, axes)

    chosen = pl.pallas_call(
        select_kernel,
        out_shape=jax.ShapeDtypeStruct((frames, packed, half), BF16),
        in_specs=[whole(), whole()],
        out_specs=whole(),
        compiler_params=params(3 * MIB + 8 * tokens * width),
        name="select",
    )(index, video)
    seen = spread(chosen, axes)

    encoded = pl.pallas_call(
        attend_kernel,
        out_shape=jax.ShapeDtypeStruct((frames, packed, half), BF16),
        in_specs=[whole()] * 4,
        out_specs=whole(),
        compiler_params=params(4 * MIB + 24 * frames * packed * width),
        name="attend",
    )(index, seen, w_qkv, w_out)
    token_rows = spread(encoded, axes)

    gained = pl.pallas_call(
        project_kernel,
        out_shape=jax.ShapeDtypeStruct((tokens, columns), BF16),
        in_specs=[whole(), whole(), whole()],
        out_specs=whole(),
        compiler_params=params(4 * MIB + 16 * tokens * columns),
        name="project",
    )(token_rows, w_proj, gain)

    def swap(values, axis, flip=1):
        pairs = [(i, i ^ flip) for i in range(lax.axis_size(axis))]
        return lax.ppermute(values, axis, pairs)

    units = w_gate.shape[1]
    part = jax.ShapeDtypeStruct((tokens, units), F32)
    sums = (part, part, jax.ShapeDtypeStruct((tokens, LANES), F32))
    work = pl.CostEstimate(
        flops=tokens * w_gate.shape[0] * units // 2,
        bytes_accessed=w_gate.shape[0] * units // 2,
        transcendentals=0,
    )

    direct = outer == DIRECT
    if direct:
        blocks = [gained, swap(gained, "outer", 1), swap(gained, "outer", 2)]
        core = swap(gained, "cores")
        mid0 = swap(jnp.stack(blocks[:2]), "mid")
        core1 = swap(blocks[1], "cores")
        blocks.append(swap(blocks[2], "outer", 1))
        mid1 = swap(blocks[2], "mid")
        mid2 = swap(blocks[3], "mid")
        core2 = swap(jnp.stack(blocks[2:]), "cores")
        both0 = swap(mid0, "cores")
        both1 = swap(jnp.stack([mid1, mid2]), "cores")
        one = [block[None] for block in blocks]
        stages = (
            ((one[0], 0, (0,)),),
            ((core[None], 1, (0,)), (one[1], 0, (1,))),
            ((core1[None], 1, (1,)), (one[2], 0, (2,))),
            ((one[3], 0, (3,)), (mid0, 2, (0, 1))),
            ((core2, 1, (2, 3)), (both0, 3, (0, 1))),
            ((mid1[None], 2, (2,)), (mid2[None], 2, (3,))),
            ((both1, 3, (2, 3)),),
        )
    else:
        line = spread(jnp.broadcast_to(gained[None], (outer,) + gained.shape), "outer")
        steps = tuple(range(outer))
        mid = swap(line, "mid")
        core, both = swap(line, "cores"), swap(mid, "cores")
        blocks = ((line, 0), (core, 1), (mid, 2), (both, 3))
        stages = tuple(((block, flip, steps),) for block, flip in blocks)
    begun = ()
    for i, stage in enumerate(stages):
        sources = tuple((flip, steps, direct) for _, flip, steps in stage)
        last = i + 1 == len(stages)
        begun = pl.pallas_call(
            functools.partial(final_kernel, sources)
            if last
            else functools.partial(partial_kernel, sources, videos),
            out_shape=jax.ShapeDtypeStruct((videos, seq, units), BF16) if last else sums,
            in_specs=[whole()] * (3 + len(stage) + len(begun)),
            out_specs=whole() if last else (whole(),) * 3,
            compiler_params=params(3 * MIB + 20 * tokens * units),
            cost_estimate=work,
            name="final" if last else "part",
        )(index, w_gate, w_up, *(block for block, _, _ in stage), *begun)
    return begun


def solution(mesh):
    groups, frames = mesh.devices.shape
    devices = mesh.devices.reshape(groups, frames // 4, 2, 2)
    split = Mesh(devices, ("groups", "outer", "mid", "cores"))
    spread = ("outer", "mid", "cores")
    in_specs = (
        P("groups", spread, None, None),
        P(),
        P(),
        P("groups", spread, None),
        P("groups", spread),
        P(None, spread),
        P(spread),
        P(None, spread),
        P(None, spread),
    )
    out_specs = P("groups", None, spread)
    return jax.shard_map(
        program, mesh=split, in_specs=in_specs, out_specs=out_specs, check_vma=False
    )
```

```python
import functools

import jax
import jax.numpy as jnp
from jax import lax
from jax.experimental import pallas as pl
from jax.experimental.pallas import tpu as pltpu
from jax.sharding import Mesh
from jax.sharding import PartitionSpec as P

HEAD_DIM = 64
TOKL = 2
KMAX = 4
LANES = 128
NORM_EPS = 1e-05
SCORE_SCALE = 0.125
DIRECT = 4
NEAR = 4
MIB = 1 << 20
COVER_FLOPS = 20_000_000_000
F32 = jnp.float32
BF16 = jnp.bfloat16


def dot32(left, right):
    return jnp.dot(left, right, preferred_element_type=F32)


def swap_halves(values):
    rows = values.shape[-2] // 2
    return jnp.concatenate([values[..., rows:, :], values[..., :rows, :]], axis=-2)


def whole(space=pltpu.VMEM):
    return pl.BlockSpec(memory_space=space)


def params(limit):
    return pltpu.CompilerParams(vmem_limit_bytes=int(limit))


def collect_kernel(counts_hbm, keep_hbm, gain_hbm, out_ref, counts_ref, keep_ref, gain_ref, sems):
    arrays = ((counts_hbm, counts_ref), (keep_hbm, keep_ref), (gain_hbm, gain_ref))
    copies = [
        pltpu.make_async_copy(source, target, sems.at[i])
        for i, (source, target) in enumerate(arrays)
    ]
    for copy in copies:
        copy.start()
    for copy in copies:
        copy.wait()
    videos = keep_ref.shape[0]
    lane = lax.broadcasted_iota(jnp.int32, (1, LANES), 1)
    counts = counts_ref[...].astype(F32)
    rows = []
    for v in range(videos):
        listed = keep_ref[v, :, :LANES].astype(F32)
        rows.append(jnp.where(lane == KMAX, counts[:, v : v + 1], listed))
    gain = gain_ref[...].astype(F32)
    if gain.shape[1] < LANES:
        fill = jnp.ones((gain.shape[0], LANES - gain.shape[1]), F32)
        gain = jnp.concatenate([gain, fill], axis=1)
    rows.append(gain)
    spare = out_ref.shape[0] - videos - gain.shape[0]
    if spare:
        rows.append(jnp.zeros((spare, LANES), F32))
    out_ref[...] = jnp.concatenate(rows, axis=0).astype(out_ref.dtype)


def index_kernel(message_ref, out_ref):
    peer = lax.broadcasted_iota(jnp.int32, (out_ref.shape[0], 1, LANES), 0).astype(F32)
    row = lax.broadcasted_iota(jnp.int32, message_ref.shape, 0)
    lane = lax.broadcasted_iota(jnp.int32, message_ref.shape, 1)
    free = jnp.logical_and(row == 0, lane == KMAX + 1)
    message = message_ref[...].astype(F32)
    out_ref[...] = jnp.where(free[None], peer, message[None]).astype(out_ref.dtype)


def select_kernel(index_ref, video_ref, out_ref):
    frames = index_ref.shape[0]
    videos, _, patches, width = video_ref.shape
    seq = frames * TOKL
    half = width // 2
    own = out_ref.shape[1] // 2
    row = lax.broadcasted_iota(jnp.int32, (frames, frames), 0)
    col = lax.broadcasted_iota(jnp.int32, (frames, frames), 1)
    before = (col < row).astype(BF16)
    token = lax.broadcasted_iota(jnp.int32, (frames, seq), 1)
    patch = lax.broadcasted_iota(jnp.int32, (frames, patches), 1).astype(F32)
    for v in range(videos):
        table = index_ref[:, v, :].astype(F32)
        count = table[:, KMAX : KMAX + 1]
        offset = dot32(before, jnp.broadcast_to(count, (frames, LANES)).astype(BF16))[:, :1]
        place = token.astype(F32) - offset
        at_token, at_patch = [], []
        for s in range(KMAX):
            live = jnp.logical_and(place == s, count > s)
            at_token.append(jnp.where(live, 1.0, 0.0))
            at_patch.append(jnp.where(table[:, s : s + 1] == patch, 1.0, 0.0))
        at_token = jnp.concatenate(at_token, axis=0).astype(BF16)
        at_patch = jnp.concatenate(at_patch, axis=0).astype(BF16)
        kept = dot32(at_patch, video_ref[v, 0]).astype(BF16)
        taken = lax.dot_general(
            at_token, kept, (((0,), (0,)), ((), ())), preferred_element_type=F32
        ).astype(BF16)
        base = v * seq
        for peer in range(base // own, (base + seq) // own):
            first = peer * own - base
            rows = taken[first : first + own]
            out_ref[peer] = jnp.concatenate([rows[:, :half], rows[:, half:]], axis=0)


def unpack(rows, own):
    packs = rows.shape[0] // (2 * own)
    token = lax.broadcasted_iota(jnp.int32, (packs * own, rows.shape[0]), 0)
    source = lax.broadcasted_iota(jnp.int32, (packs * own, rows.shape[0]), 1)
    first = (token // own) * (2 * own) + token % own
    low = dot32(jnp.where(source == first, 1.0, 0.0).astype(BF16), rows)
    high = dot32(jnp.where(source == first + own, 1.0, 0.0).astype(BF16), rows)
    return low, high


def attend_kernel(index_ref, rows_ref, w_qkv_ref, w_out_ref, out_ref):
    frames, packed, half = rows_ref.shape
    own = packed // 2
    width = 2 * half
    seq = frames * TOKL
    videos = frames * own // seq
    low, high = unpack(rows_ref[...].reshape(frames * packed, half), own)
    raw = jnp.concatenate([low, high], axis=1)
    centred = raw - jnp.mean(raw, axis=1, keepdims=True)
    variance = jnp.mean(centred * centred, axis=1, keepdims=True)
    normed = (centred * lax.rsqrt(variance + NORM_EPS)).astype(BF16)

    pairs = frames * own // packed

    def project(start):
        part = dot32(normed, w_qkv_ref[:, start : start + width])
        return part.astype(BF16).astype(F32).reshape(pairs, packed, width)

    table = index_ref[...].astype(F32)
    row = lax.broadcasted_iota(jnp.int32, (1, packed, LANES), 1)
    upper = row >= own
    me = table[:1, :1, KMAX + 1 : KMAX + 2].astype(jnp.int32)
    flat = me * own + jnp.where(upper, row - own, row)
    owner = jnp.zeros((pairs, packed, LANES), F32)
    for v in range(videos):
        count = table[:, v : v + 1, KMAX : KMAX + 1]
        upto = count
        step = 1
        while step < frames:
            moved = jnp.concatenate([jnp.zeros((step, 1, 1), F32), upto[:-step]], axis=0)
            upto = upto + moved
            step *= 2
        place = (flat - v * seq).astype(F32)
        ours = jnp.logical_and(flat >= v * seq, flat < (v + 1) * seq)
        below = upto - count
        below = below.reshape(pairs, 2, 1, 1)
        upto = upto.reshape(pairs, 2, 1, 1)
        start = jnp.where(upper, below[:, 1], below[:, 0])
        stop = jnp.where(upper, upto[:, 1], upto[:, 0])
        inside = jnp.logical_and(place >= start, place < stop)
        owner = owner + jnp.where(jnp.logical_and(inside, ours), 1.0, 0.0)
    owner = owner[:, :, :1]

    def over_frames(values):
        total = jnp.sum(values, axis=0)
        return total + swap_halves(total)

    query = over_frames(project(0) * owner)
    product = (project(width) * query[None]).reshape(-1, width)
    feature = lax.broadcasted_iota(jnp.int32, (width, LANES), 0) // HEAD_DIM
    head = lax.broadcasted_iota(jnp.int32, (width, LANES), 1)
    to_head = jnp.where(feature == head, 1.0, 0.0).astype(BF16)
    coarse = product.astype(BF16)
    rest = product - coarse.astype(F32)
    fine = rest.astype(BF16)
    last = (rest - fine.astype(F32)).astype(BF16)
    scores = dot32(jnp.concatenate([coarse, fine, last], axis=0), to_head)
    scores = jnp.sum(scores.reshape(3, pairs, packed, LANES), axis=0) * SCORE_SCALE
    largest = jnp.max(scores, axis=0)
    largest = jnp.maximum(largest, swap_halves(largest))
    raised = jnp.exp(scores - largest[None])
    weights = (raised / over_frames(raised)[None]).astype(BF16)
    head = lax.broadcasted_iota(jnp.int32, (LANES, width), 0)
    feature = lax.broadcasted_iota(jnp.int32, (LANES, width), 1) // HEAD_DIM
    from_head = jnp.where(feature == head, 1.0, 0.0).astype(BF16)
    spread = dot32(weights.reshape(-1, LANES), from_head).reshape(pairs, packed, width)
    attended = over_frames(spread * project(2 * width)).astype(BF16)
    change = dot32(attended, w_out_ref[...])
    residual = over_frames(raw.reshape(pairs, packed, width) * owner)
    encoded = residual + change
    place = lax.broadcasted_iota(jnp.int32, (packed, half), 0)
    encoded = jnp.where(place < own, encoded[:, :half], encoded[:, half:]).astype(BF16)
    out_ref[...] = jnp.broadcast_to(encoded[None], out_ref.shape)


def project_kernel(rows_ref, w_proj_ref, gain_ref, out_ref):
    frames, packed, half = rows_ref.shape
    own = packed // 2
    rows = rows_ref[...].reshape(frames * packed, half)
    low, high = (part.astype(BF16) for part in unpack(rows, own))
    total = dot32(low, w_proj_ref[:half, :]) + dot32(high, w_proj_ref[half:, :])
    gain = gain_ref[...].astype(F32)
    lanes = gain.shape[1]
    for r in range(gain.shape[0]):
        piece = slice(r * lanes, (r + 1) * lanes)
        gained = (total[:, piece] * gain[r : r + 1]).astype(BF16)
        out_ref[:, piece] = gained


def places(index_ref, sources):
    me = jnp.max(index_ref[0, :1, KMAX + 1 : KMAX + 2].astype(F32)).astype(jnp.int32)
    row = me // NEAR
    found = []
    for flip, steps, direct in sources:
        near = jnp.bitwise_xor(me - row * NEAR, flip)
        for i, step in enumerate(steps):
            outer = jnp.bitwise_xor(row, step) if direct else step
            found.append((i, outer * NEAR + near))
    return found


def square_sums(blocks, videos, index_ref):
    tokens, columns = blocks[0][0].shape[1:]
    gain_rows = -(-columns // LANES)
    squares = jnp.zeros((tokens, LANES), F32)
    for rows_ref, i, place in blocks:
        inverse = 1.0 / index_ref[place].astype(F32)[videos : videos + gain_rows]
        for r in range(gain_rows):
            piece = rows_ref[i, :, r * LANES : min((r + 1) * LANES, columns)].astype(F32)
            piece = piece * inverse[r : r + 1, : piece.shape[1]]
            piece = piece * piece
            if piece.shape[1] < LANES:
                fill = jnp.zeros((tokens, LANES - piece.shape[1]), F32)
                piece = jnp.concatenate([piece, fill], axis=1)
            squares = squares + piece
    return squares


def products(blocks, w_gate_ref, w_up_ref, begun, emit):
    columns = blocks[0][0].shape[2]
    width = w_gate_ref.shape[1]
    block = min(width, 256)
    for first in range(0, width, block):
        sums = []
        for i, w_ref in enumerate((w_gate_ref, w_up_ref)):
            total = begun[i][:, first : first + block] if begun else None
            for rows_ref, part, place in blocks:
                depth = pl.ds(pl.multiple_of(place * columns, columns), columns)
                one = dot32(rows_ref[part], w_ref[depth, first : first + block])
                total = one if total is None else total + one
            sums.append(total)
        emit(first, block, *sums)


def split_refs(sources, refs):
    index_ref, w_gate_ref, w_up_ref = refs[:3]
    rows = refs[3 : 3 + len(sources)]
    owners = [ref for ref, source in zip(rows, sources) for _ in source[1]]
    blocks = [(ref,) + found for ref, found in zip(owners, places(index_ref, sources))]
    return index_ref, w_gate_ref, w_up_ref, blocks, refs[3 + len(sources) :]


def partial_kernel(sources, videos, *refs):
    index_ref, w_gate_ref, w_up_ref, blocks, rest = split_refs(sources, refs)
    begun, (gate_ref, up_ref, squares_ref) = rest[:-3], rest[-3:]

    def emit(first, block, gate, up):
        gate_ref[:, first : first + block] = gate
        up_ref[:, first : first + block] = up

    squares = square_sums(blocks, videos, index_ref)
    squares_ref[...] = squares + begun[2][...] if begun else squares
    products(blocks, w_gate_ref, w_up_ref, begun, emit)


def final_kernel(sources, *refs):
    index_ref, w_gate_ref, w_up_ref, blocks, rest = split_refs(sources, refs)
    begun, out_ref = rest[:3], rest[3]
    videos = out_ref.shape[0]
    squares = begun[2][...] + square_sums(blocks, videos, index_ref)
    mean = jnp.sum(squares, axis=1, keepdims=True) / w_gate_ref.shape[0]
    scale = lax.rsqrt(mean + NORM_EPS)

    def emit(first, block, gate, up):
        hidden = (jax.nn.silu(gate * scale) * (up * scale)).astype(BF16)
        out_ref[:, :, first : first + block] = hidden.reshape(videos, -1, block)

    products(blocks, w_gate_ref, w_up_ref, begun, emit)


def program(video, w_qkv, w_out, keep_list, kept_counts, w_proj, llm_gain, w_gate, w_up):
    videos, _, patches, width = video.shape
    axes = ("outer", "mid", "cores")
    frames, outer = lax.axis_size(axes), lax.axis_size("outer")
    seq = frames * TOKL
    tokens = videos * seq
    packed = 2 * (tokens // frames)
    half = width // 2
    columns = w_proj.shape[1]
    spread = functools.partial(lax.all_to_all, split_axis=0, concat_axis=0, tiled=True)
    gain_rows = -(-columns // LANES)
    gain = llm_gain.reshape(gain_rows, -1)

    counts, listed = kept_counts.T, keep_list
    kind = BF16 if max(patches, frames) <= 256 else F32
    rows = -(-(videos + gain_rows) // 8) * 8
    message = pl.pallas_call(
        collect_kernel,
        out_shape=jax.ShapeDtypeStruct((rows, LANES), kind),
        in_specs=[whole(pltpu.HBM)] * 3,
        out_specs=whole(),
        scratch_shapes=[pltpu.VMEM(x.shape, x.dtype) for x in (counts, listed, gain)]
        + [pltpu.SemaphoreType.DMA((3,))],
        compiler_params=params(2 * MIB),
        name="collect",
    )(*(pltpu.with_memory_space_constraint(x, pltpu.HBM) for x in (counts, listed, gain)))
    message = pl.pallas_call(
        index_kernel,
        out_shape=jax.ShapeDtypeStruct((frames, rows, LANES), kind),
        in_specs=[whole()],
        out_specs=whole(),
        compiler_params=params(2 * MIB),
        cost_estimate=pl.CostEstimate(flops=COVER_FLOPS, bytes_accessed=65536, transcendentals=0),
        name="index",
    )(message)
    index = spread(message, axes)

    chosen = pl.pallas_call(
        select_kernel,
        out_shape=jax.ShapeDtypeStruct((frames, packed, half), BF16),
        in_specs=[whole(), whole()],
        out_specs=whole(),
        compiler_params=params(3 * MIB + 8 * tokens * width),
        name="select",
    )(index, video)
    seen = spread(chosen, axes)

    encoded = pl.pallas_call(
        attend_kernel,
        out_shape=jax.ShapeDtypeStruct((frames, packed, half), BF16),
        in_specs=[whole()] * 4,
        out_specs=whole(),
        compiler_params=params(4 * MIB + 24 * frames * packed * width),
        name="attend",
    )(index, seen, w_qkv, w_out)
    token_rows = spread(encoded, axes)

    gained = pl.pallas_call(
        project_kernel,
        out_shape=jax.ShapeDtypeStruct((tokens, columns), BF16),
        in_specs=[whole(), whole(), whole()],
        out_specs=whole(),
        compiler_params=params(4 * MIB + 16 * tokens * columns),
        name="project",
    )(token_rows, w_proj, gain)

    def swap(values, axis, flip=1):
        pairs = [(i, i ^ flip) for i in range(lax.axis_size(axis))]
        return lax.ppermute(values, axis, pairs)

    units = w_gate.shape[1]
    part = jax.ShapeDtypeStruct((tokens, units), F32)
    sums = (part, part, jax.ShapeDtypeStruct((tokens, LANES), F32))
    work = pl.CostEstimate(
        flops=tokens * w_gate.shape[0] * units // 2,
        bytes_accessed=w_gate.shape[0] * units // 2,
        transcendentals=0,
    )

    direct = outer == DIRECT
    if direct:
        blocks = [gained] + [swap(gained, "outer", k) for k in range(1, outer)]
        near, rest = jnp.stack(blocks[:2]), jnp.stack(blocks[2:])
        mid0, mid1 = swap(near, "mid"), swap(rest, "mid")
        core0, core1 = swap(near, "cores"), swap(rest, "cores")
        both0, both1 = swap(mid0, "cores"), swap(mid1, "cores")
        first, second = (0, 1), (2, 3)
        stages = (
            ((near, 0, first),),
            ((core0, 1, first),),
            ((rest, 0, second),),
            ((core1, 1, second), (mid0, 2, first),),
            ((both0, 3, first),),
            ((mid1, 2, second),),
            ((both1, 3, second),),
        )
    else:
        line = spread(jnp.broadcast_to(gained[None], (outer,) + gained.shape), "outer")
        steps = tuple(range(outer))
        mid = swap(line, "mid")
        core, both = swap(line, "cores"), swap(mid, "cores")
        blocks = ((line, 0), (core, 1), (mid, 2), (both, 3))
        stages = tuple(((block, flip, steps),) for block, flip in blocks)
    begun = ()
    for i, stage in enumerate(stages):
        sources = tuple((flip, steps, direct) for _, flip, steps in stage)
        last = i + 1 == len(stages)
        begun = pl.pallas_call(
            functools.partial(final_kernel, sources)
            if last
            else functools.partial(partial_kernel, sources, videos),
            out_shape=jax.ShapeDtypeStruct((videos, seq, units), BF16) if last else sums,
            in_specs=[whole()] * (3 + len(stage) + len(begun)),
            out_specs=whole() if last else (whole(),) * 3,
            compiler_params=params(3 * MIB + 20 * tokens * units),
            cost_estimate=work,
            name="final" if last else "part",
        )(index, w_gate, w_up, *(block for block, _, _ in stage), *begun)
    return begun


def solution(mesh):
    groups, frames = mesh.devices.shape
    devices = mesh.devices.reshape(groups, frames // 4, 2, 2)
    split = Mesh(devices, ("groups", "outer", "mid", "cores"))
    spread = ("outer", "mid", "cores")
    in_specs = (
        P("groups", spread, None, None),
        P(),
        P(),
        P("groups", spread, None),
        P("groups", spread),
        P(None, spread),
        P(spread),
        P(None, spread),
        P(None, spread),
    )
    out_specs = P("groups", None, spread)
    return jax.shard_map(
        program, mesh=split, in_specs=in_specs, out_specs=out_specs, check_vma=False
    )
```

```python
import functools

import jax
import jax.numpy as jnp
from jax import lax
from jax.experimental import pallas as pl
from jax.experimental.pallas import tpu as pltpu
from jax.sharding import Mesh
from jax.sharding import PartitionSpec as P

HEAD_DIM = 64
TOKL = 2
KMAX = 4
LANES = 128
NORM_EPS = 1e-05
SCORE_SCALE = 0.125
DIRECT = 4
NEAR = 4
BLOCK = 256
WIDE = 1024
MIB = 1 << 20
COVER_FLOPS = 20_000_000_000
F32 = jnp.float32
BF16 = jnp.bfloat16


def dot32(left, right):
    return jnp.dot(left, right, preferred_element_type=F32)


def swap_halves(values):
    rows = values.shape[-2] // 2
    return jnp.concatenate([values[..., rows:, :], values[..., :rows, :]], axis=-2)


def whole(space=pltpu.VMEM):
    return pl.BlockSpec(memory_space=space)


def params(limit):
    return pltpu.CompilerParams(vmem_limit_bytes=int(limit))


def collect_kernel(counts_hbm, keep_hbm, gain_hbm, out_ref, counts_ref, keep_ref, gain_ref, sems):
    arrays = ((counts_hbm, counts_ref), (keep_hbm, keep_ref), (gain_hbm, gain_ref))
    copies = [
        pltpu.make_async_copy(source, target, sems.at[i])
        for i, (source, target) in enumerate(arrays)
    ]
    for copy in copies:
        copy.start()
    for copy in copies:
        copy.wait()
    videos = keep_ref.shape[0]
    lane = lax.broadcasted_iota(jnp.int32, (1, LANES), 1)
    counts = counts_ref[...].astype(F32)
    rows = []
    for v in range(videos):
        listed = keep_ref[v, :, :LANES].astype(F32)
        rows.append(jnp.where(lane == KMAX, counts[:, v : v + 1], listed))
    gain = gain_ref[...].astype(F32)
    if gain.shape[1] < LANES:
        fill = jnp.ones((gain.shape[0], LANES - gain.shape[1]), F32)
        gain = jnp.concatenate([gain, fill], axis=1)
    rows.append(gain)
    spare = out_ref.shape[0] - videos - gain.shape[0]
    if spare:
        rows.append(jnp.zeros((spare, LANES), F32))
    out_ref[...] = jnp.concatenate(rows, axis=0).astype(out_ref.dtype)


def index_kernel(message_ref, out_ref):
    peer = lax.broadcasted_iota(jnp.int32, (out_ref.shape[0], 1, LANES), 0).astype(F32)
    row = lax.broadcasted_iota(jnp.int32, message_ref.shape, 0)
    lane = lax.broadcasted_iota(jnp.int32, message_ref.shape, 1)
    free = jnp.logical_and(row == 0, lane == KMAX + 1)
    message = message_ref[...].astype(F32)
    out_ref[...] = jnp.where(free[None], peer, message[None]).astype(out_ref.dtype)


def select_kernel(index_ref, video_ref, out_ref):
    frames = index_ref.shape[0]
    videos, _, patches, width = video_ref.shape
    seq = frames * TOKL
    half = width // 2
    own = out_ref.shape[1] // 2
    row = lax.broadcasted_iota(jnp.int32, (frames, frames), 0)
    col = lax.broadcasted_iota(jnp.int32, (frames, frames), 1)
    before = (col < row).astype(BF16)
    token = lax.broadcasted_iota(jnp.int32, (frames, seq), 1)
    patch = lax.broadcasted_iota(jnp.int32, (frames, patches), 1).astype(F32)
    for v in range(videos):
        table = index_ref[:, v, :].astype(F32)
        count = table[:, KMAX : KMAX + 1]
        offset = dot32(before, jnp.broadcast_to(count, (frames, LANES)).astype(BF16))[:, :1]
        place = token.astype(F32) - offset
        at_token, at_patch = [], []
        for s in range(KMAX):
            live = jnp.logical_and(place == s, count > s)
            at_token.append(jnp.where(live, 1.0, 0.0))
            at_patch.append(jnp.where(table[:, s : s + 1] == patch, 1.0, 0.0))
        at_token = jnp.concatenate(at_token, axis=0).astype(BF16)
        at_patch = jnp.concatenate(at_patch, axis=0).astype(BF16)
        kept = dot32(at_patch, video_ref[v, 0]).astype(BF16)
        taken = lax.dot_general(
            at_token, kept, (((0,), (0,)), ((), ())), preferred_element_type=F32
        ).astype(BF16)
        base = v * seq
        for peer in range(base // own, (base + seq) // own):
            first = peer * own - base
            rows = taken[first : first + own]
            out_ref[peer] = jnp.concatenate([rows[:, :half], rows[:, half:]], axis=0)


def unpack(rows, own):
    packs = rows.shape[0] // (2 * own)
    token = lax.broadcasted_iota(jnp.int32, (packs * own, rows.shape[0]), 0)
    source = lax.broadcasted_iota(jnp.int32, (packs * own, rows.shape[0]), 1)
    first = (token // own) * (2 * own) + token % own
    low = dot32(jnp.where(source == first, 1.0, 0.0).astype(BF16), rows)
    high = dot32(jnp.where(source == first + own, 1.0, 0.0).astype(BF16), rows)
    return low, high


def attend_kernel(index_ref, rows_ref, w_qkv_ref, w_out_ref, out_ref):
    frames, packed, half = rows_ref.shape
    own = packed // 2
    width = 2 * half
    seq = frames * TOKL
    videos = frames * own // seq
    low, high = unpack(rows_ref[...].reshape(frames * packed, half), own)
    raw = jnp.concatenate([low, high], axis=1)
    centred = raw - jnp.mean(raw, axis=1, keepdims=True)
    variance = jnp.mean(centred * centred, axis=1, keepdims=True)
    normed = (centred * lax.rsqrt(variance + NORM_EPS)).astype(BF16)

    pairs = frames * own // packed

    def project(start):
        part = dot32(normed, w_qkv_ref[:, start : start + width])
        return part.astype(BF16).astype(F32).reshape(pairs, packed, width)

    table = index_ref[...].astype(F32)
    row = lax.broadcasted_iota(jnp.int32, (1, packed, LANES), 1)
    upper = row >= own
    me = table[:1, :1, KMAX + 1 : KMAX + 2].astype(jnp.int32)
    flat = me * own + jnp.where(upper, row - own, row)
    owner = jnp.zeros((pairs, packed, LANES), F32)
    for v in range(videos):
        count = table[:, v : v + 1, KMAX : KMAX + 1]
        upto = count
        step = 1
        while step < frames:
            moved = jnp.concatenate([jnp.zeros((step, 1, 1), F32), upto[:-step]], axis=0)
            upto = upto + moved
            step *= 2
        place = (flat - v * seq).astype(F32)
        ours = jnp.logical_and(flat >= v * seq, flat < (v + 1) * seq)
        below = upto - count
        below = below.reshape(pairs, 2, 1, 1)
        upto = upto.reshape(pairs, 2, 1, 1)
        start = jnp.where(upper, below[:, 1], below[:, 0])
        stop = jnp.where(upper, upto[:, 1], upto[:, 0])
        inside = jnp.logical_and(place >= start, place < stop)
        owner = owner + jnp.where(jnp.logical_and(inside, ours), 1.0, 0.0)
    owner = owner[:, :, :1]

    def over_frames(values):
        total = jnp.sum(values, axis=0)
        return total + swap_halves(total)

    query = over_frames(project(0) * owner)
    product = (project(width) * query[None]).reshape(-1, width)
    feature = lax.broadcasted_iota(jnp.int32, (width, LANES), 0) // HEAD_DIM
    head = lax.broadcasted_iota(jnp.int32, (width, LANES), 1)
    to_head = jnp.where(feature == head, 1.0, 0.0).astype(BF16)
    coarse = product.astype(BF16)
    rest = product - coarse.astype(F32)
    fine = rest.astype(BF16)
    last = (rest - fine.astype(F32)).astype(BF16)
    scores = dot32(jnp.concatenate([coarse, fine, last], axis=0), to_head)
    scores = jnp.sum(scores.reshape(3, pairs, packed, LANES), axis=0) * SCORE_SCALE
    largest = jnp.max(scores, axis=0)
    largest = jnp.maximum(largest, swap_halves(largest))
    raised = jnp.exp(scores - largest[None])
    weights = (raised / over_frames(raised)[None]).astype(BF16)
    head = lax.broadcasted_iota(jnp.int32, (LANES, width), 0)
    feature = lax.broadcasted_iota(jnp.int32, (LANES, width), 1) // HEAD_DIM
    from_head = jnp.where(feature == head, 1.0, 0.0).astype(BF16)
    spread = dot32(weights.reshape(-1, LANES), from_head).reshape(pairs, packed, width)
    attended = over_frames(spread * project(2 * width)).astype(BF16)
    change = dot32(attended, w_out_ref[...])
    residual = over_frames(raw.reshape(pairs, packed, width) * owner)
    encoded = residual + change
    place = lax.broadcasted_iota(jnp.int32, (packed, half), 0)
    encoded = jnp.where(place < own, encoded[:, :half], encoded[:, half:]).astype(BF16)
    out_ref[...] = jnp.broadcast_to(encoded[None], out_ref.shape)


def project_kernel(rows_ref, w_proj_ref, gain_ref, out_ref):
    frames, packed, half = rows_ref.shape
    own = packed // 2
    rows = rows_ref[...].reshape(frames * packed, half)
    low, high = (part.astype(BF16) for part in unpack(rows, own))
    total = dot32(low, w_proj_ref[:half, :]) + dot32(high, w_proj_ref[half:, :])
    gain = gain_ref[...].astype(F32)
    lanes = gain.shape[1]
    for r in range(gain.shape[0]):
        piece = slice(r * lanes, (r + 1) * lanes)
        gained = (total[:, piece] * gain[r : r + 1]).astype(BF16)
        out_ref[:, piece] = gained


def places(index_ref, sources):
    me = jnp.max(index_ref[0, :1, KMAX + 1 : KMAX + 2].astype(F32)).astype(jnp.int32)
    row = me // NEAR
    found = []
    for flip, steps, direct in sources:
        near = jnp.bitwise_xor(me - row * NEAR, flip)
        for i, step in enumerate(steps):
            outer = jnp.bitwise_xor(row, step) if direct else step
            found.append((i, outer * NEAR + near))
    return found


def square_sums(blocks, videos, index_ref):
    tokens, columns = blocks[0][0].shape[1:]
    gain_rows = -(-columns // LANES)
    squares = jnp.zeros((tokens, LANES), F32)
    for rows_ref, i, place in blocks:
        inverse = 1.0 / index_ref[place].astype(F32)[videos : videos + gain_rows]
        for r in range(gain_rows):
            piece = rows_ref[i, :, r * LANES : min((r + 1) * LANES, columns)].astype(F32)
            piece = piece * inverse[r : r + 1, : piece.shape[1]]
            piece = piece * piece
            if piece.shape[1] < LANES:
                fill = jnp.zeros((tokens, LANES - piece.shape[1]), F32)
                piece = jnp.concatenate([piece, fill], axis=1)
            squares = squares + piece
    return squares


def products(blocks, w_gate_ref, w_up_ref, begun, emit, limit):
    columns = blocks[0][0].shape[2]
    width = w_gate_ref.shape[1]
    block = min(width, limit)
    for first in range(0, width, block):
        sums = []
        for i, w_ref in enumerate((w_gate_ref, w_up_ref)):
            total = begun[i][:, first : first + block] if begun else None
            for rows_ref, part, place in blocks:
                depth = pl.ds(pl.multiple_of(place * columns, columns), columns)
                one = dot32(rows_ref[part], w_ref[depth, first : first + block])
                total = one if total is None else total + one
            sums.append(total)
        emit(first, block, *sums)


def split_refs(sources, refs):
    index_ref, w_gate_ref, w_up_ref = refs[:3]
    rows = refs[3 : 3 + len(sources)]
    owners = [ref for ref, source in zip(rows, sources) for _ in source[1]]
    blocks = [(ref,) + found for ref, found in zip(owners, places(index_ref, sources))]
    return index_ref, w_gate_ref, w_up_ref, blocks, refs[3 + len(sources) :]


def partial_kernel(sources, videos, *refs):
    index_ref, w_gate_ref, w_up_ref, blocks, rest = split_refs(sources, refs)
    begun, (gate_ref, up_ref, squares_ref) = rest[:-3], rest[-3:]

    def emit(first, block, gate, up):
        gate_ref[:, first : first + block] = gate
        up_ref[:, first : first + block] = up

    squares = square_sums(blocks, videos, index_ref)
    squares_ref[...] = squares + begun[2][...] if begun else squares
    products(blocks, w_gate_ref, w_up_ref, begun, emit, WIDE)


def final_kernel(sources, *refs):
    refs, (hidden_ref, sems) = refs[:-2], refs[-2:]
    index_ref, w_gate_ref, w_up_ref, blocks, rest = split_refs(sources, refs)
    begun, out_hbm = rest[:3], rest[3]
    videos = hidden_ref.shape[0]
    squares = begun[2][...] + square_sums(blocks, videos, index_ref)
    mean = jnp.sum(squares, axis=1, keepdims=True) / w_gate_ref.shape[0]
    scale = lax.rsqrt(mean + NORM_EPS)
    copies = []

    def emit(first, block, gate, up):
        hidden = (jax.nn.silu(gate * scale) * (up * scale)).astype(BF16)
        units = slice(first, first + block)
        hidden_ref[:, :, units] = hidden.reshape(videos, -1, block)
        copy = pltpu.make_async_copy(
            hidden_ref.at[:, :, units], out_hbm.at[:, :, units], sems.at[len(copies)]
        )
        copy.start()
        copies.append(copy)

    products(blocks, w_gate_ref, w_up_ref, begun, emit, BLOCK)
    for copy in copies:
        copy.wait()


def program(video, w_qkv, w_out, keep_list, kept_counts, w_proj, llm_gain, w_gate, w_up):
    videos, _, patches, width = video.shape
    axes = ("outer", "mid", "cores")
    frames, outer = lax.axis_size(axes), lax.axis_size("outer")
    seq = frames * TOKL
    tokens = videos * seq
    packed = 2 * (tokens // frames)
    half = width // 2
    columns = w_proj.shape[1]
    spread = functools.partial(lax.all_to_all, split_axis=0, concat_axis=0, tiled=True)
    gain_rows = -(-columns // LANES)
    gain = llm_gain.reshape(gain_rows, -1)

    counts, listed = kept_counts.T, keep_list
    kind = BF16 if max(patches, frames) <= 256 else F32
    rows = -(-(videos + gain_rows) // 8) * 8
    message = pl.pallas_call(
        collect_kernel,
        out_shape=jax.ShapeDtypeStruct((rows, LANES), kind),
        in_specs=[whole(pltpu.HBM)] * 3,
        out_specs=whole(),
        scratch_shapes=[pltpu.VMEM(x.shape, x.dtype) for x in (counts, listed, gain)]
        + [pltpu.SemaphoreType.DMA((3,))],
        compiler_params=params(2 * MIB),
        name="collect",
    )(*(pltpu.with_memory_space_constraint(x, pltpu.HBM) for x in (counts, listed, gain)))
    message = pl.pallas_call(
        index_kernel,
        out_shape=jax.ShapeDtypeStruct((frames, rows, LANES), kind),
        in_specs=[whole()],
        out_specs=whole(),
        compiler_params=params(2 * MIB),
        cost_estimate=pl.CostEstimate(flops=COVER_FLOPS, bytes_accessed=65536, transcendentals=0),
        name="index",
    )(message)
    index = spread(message, axes)

    chosen = pl.pallas_call(
        select_kernel,
        out_shape=jax.ShapeDtypeStruct((frames, packed, half), BF16),
        in_specs=[whole(), whole()],
        out_specs=whole(),
        compiler_params=params(3 * MIB + 8 * tokens * width),
        name="select",
    )(index, video)
    seen = spread(chosen, axes)

    encoded = pl.pallas_call(
        attend_kernel,
        out_shape=jax.ShapeDtypeStruct((frames, packed, half), BF16),
        in_specs=[whole()] * 4,
        out_specs=whole(),
        compiler_params=params(4 * MIB + 24 * frames * packed * width),
        name="attend",
    )(index, seen, w_qkv, w_out)
    token_rows = spread(encoded, axes)

    gained = pl.pallas_call(
        project_kernel,
        out_shape=jax.ShapeDtypeStruct((tokens, columns), BF16),
        in_specs=[whole(), whole(), whole()],
        out_specs=whole(),
        compiler_params=params(4 * MIB + 16 * tokens * columns),
        name="project",
    )(token_rows, w_proj, gain)

    def swap(values, axis, flip=1):
        pairs = [(i, i ^ flip) for i in range(lax.axis_size(axis))]
        return lax.ppermute(values, axis, pairs)

    units = w_gate.shape[1]
    part = jax.ShapeDtypeStruct((tokens, units), F32)
    sums = (part, part, jax.ShapeDtypeStruct((tokens, LANES), F32))
    work = pl.CostEstimate(
        flops=tokens * w_gate.shape[0] * units // 2,
        bytes_accessed=w_gate.shape[0] * units // 2,
        transcendentals=0,
    )

    direct = outer == DIRECT
    if direct:
        blocks = [gained] + [swap(gained, "outer", k) for k in range(1, outer)]
        near, rest = jnp.stack(blocks[:2]), jnp.stack(blocks[2:])
        mid0, mid1 = swap(near, "mid"), swap(rest, "mid")
        core0, core1 = swap(near, "cores"), swap(rest, "cores")
        both0, both1 = swap(mid0, "cores"), swap(mid1, "cores")
        first, second = (0, 1), (2, 3)
        stages = (
            ((near, 0, first),),
            ((core0, 1, first),),
            ((rest, 0, second),),
            ((core1, 1, second), (mid0, 2, first),),
            ((both0, 3, first),),
            ((mid1, 2, second),),
            ((both1, 3, second),),
        )
    else:
        line = spread(jnp.broadcast_to(gained[None], (outer,) + gained.shape), "outer")
        steps = tuple(range(outer))
        mid = swap(line, "mid")
        core, both = swap(line, "cores"), swap(mid, "cores")
        blocks = ((line, 0), (core, 1), (mid, 2), (both, 3))
        stages = tuple(((block, flip, steps),) for block, flip in blocks)
    begun = ()
    for i, stage in enumerate(stages):
        sources = tuple((flip, steps, direct) for _, flip, steps in stage)
        last = i + 1 == len(stages)
        begun = pl.pallas_call(
            functools.partial(final_kernel, sources)
            if last
            else functools.partial(partial_kernel, sources, videos),
            out_shape=jax.ShapeDtypeStruct((videos, seq, units), BF16) if last else sums,
            in_specs=[whole()] * (3 + len(stage) + len(begun)),
            out_specs=whole(pl.ANY) if last else (whole(),) * 3,
            scratch_shapes=[
                pltpu.VMEM((videos, seq, units), BF16),
                pltpu.SemaphoreType.DMA((-(-units // BLOCK),)),
            ]
            if last
            else [],
            compiler_params=params(3 * MIB + 20 * tokens * units),
            cost_estimate=work,
            name="final" if last else "part",
        )(index, w_gate, w_up, *(block for block, _, _ in stage), *begun)
    return begun


def solution(mesh):
    groups, frames = mesh.devices.shape
    devices = mesh.devices.reshape(groups, frames // 4, 2, 2)
    split = Mesh(devices, ("groups", "outer", "mid", "cores"))
    spread = ("outer", "mid", "cores")
    in_specs = (
        P("groups", spread, None, None),
        P(),
        P(),
        P("groups", spread, None),
        P("groups", spread),
        P(None, spread),
        P(spread),
        P(None, spread),
        P(None, spread),
    )
    out_specs = P("groups", None, spread)
    return jax.shard_map(
        program, mesh=split, in_specs=in_specs, out_specs=out_specs, check_vma=False
    )
```

```python
import functools

import jax
import jax.numpy as jnp
from jax import lax
from jax.experimental import pallas as pl
from jax.experimental.pallas import tpu as pltpu
from jax.sharding import Mesh
from jax.sharding import PartitionSpec as P

HEAD_DIM = 64
TOKL = 2
KMAX = 4
LANES = 128
NORM_EPS = 1e-05
SCORE_SCALE = 0.125
DIRECT = 4
NEAR = 4
BLOCK = 256
WIDE = 1024
MIB = 1 << 20
COVER_FLOPS = 20_000_000_000
F32 = jnp.float32
BF16 = jnp.bfloat16


def dot32(left, right):
    return jnp.dot(left, right, preferred_element_type=F32)


def swap_halves(values):
    rows = values.shape[-2] // 2
    return jnp.concatenate([values[..., rows:, :], values[..., :rows, :]], axis=-2)


def whole(space=pltpu.VMEM):
    return pl.BlockSpec(memory_space=space)


def params(limit):
    return pltpu.CompilerParams(vmem_limit_bytes=int(limit))


def index_kernel(counts_hbm, keep_hbm, gain_hbm, out_ref, counts_ref, keep_ref, gain_ref, sems):
    arrays = ((counts_hbm, counts_ref), (keep_hbm, keep_ref), (gain_hbm, gain_ref))
    copies = [
        pltpu.make_async_copy(source, target, sems.at[i])
        for i, (source, target) in enumerate(arrays)
    ]
    for copy in copies:
        copy.start()
    for copy in copies:
        copy.wait()
    videos = keep_ref.shape[0]
    peers, height, _ = out_ref.shape
    lane = lax.broadcasted_iota(jnp.int32, (1, LANES), 1)
    counts = counts_ref[...].astype(F32)
    rows = []
    for v in range(videos):
        listed = keep_ref[v, :, :LANES].astype(F32)
        rows.append(jnp.where(lane == KMAX, counts[:, v : v + 1], listed))
    gain = gain_ref[...].astype(F32)
    if gain.shape[1] < LANES:
        fill = jnp.ones((gain.shape[0], LANES - gain.shape[1]), F32)
        gain = jnp.concatenate([gain, fill], axis=1)
    rows.append(gain)
    spare = height - videos - gain.shape[0]
    if spare:
        rows.append(jnp.zeros((spare, LANES), F32))
    message = jnp.concatenate(rows, axis=0)
    peer = lax.broadcasted_iota(jnp.int32, (peers, 1, LANES), 0).astype(F32)
    row = lax.broadcasted_iota(jnp.int32, (height, LANES), 0)
    lane = lax.broadcasted_iota(jnp.int32, (height, LANES), 1)
    free = jnp.logical_and(row == 0, lane == KMAX + 1)
    out_ref[...] = jnp.where(free[None], peer, message[None]).astype(out_ref.dtype)


def select_kernel(index_ref, video_ref, out_ref):
    frames = index_ref.shape[0]
    videos, _, patches, width = video_ref.shape
    seq = frames * TOKL
    half = width // 2
    own = out_ref.shape[1] // 2
    row = lax.broadcasted_iota(jnp.int32, (frames, frames), 0)
    col = lax.broadcasted_iota(jnp.int32, (frames, frames), 1)
    before = (col < row).astype(BF16)
    token = lax.broadcasted_iota(jnp.int32, (frames, seq), 1)
    patch = lax.broadcasted_iota(jnp.int32, (frames, patches), 1).astype(F32)
    for v in range(videos):
        table = index_ref[:, v, :].astype(F32)
        count = table[:, KMAX : KMAX + 1]
        offset = dot32(before, jnp.broadcast_to(count, (frames, LANES)).astype(BF16))[:, :1]
        place = token.astype(F32) - offset
        at_token, at_patch = [], []
        for s in range(KMAX):
            live = jnp.logical_and(place == s, count > s)
            at_token.append(jnp.where(live, 1.0, 0.0))
            at_patch.append(jnp.where(table[:, s : s + 1] == patch, 1.0, 0.0))
        at_token = jnp.concatenate(at_token, axis=0).astype(BF16)
        at_patch = jnp.concatenate(at_patch, axis=0).astype(BF16)
        kept = dot32(at_patch, video_ref[v, 0]).astype(BF16)
        taken = lax.dot_general(
            at_token, kept, (((0,), (0,)), ((), ())), preferred_element_type=F32
        ).astype(BF16)
        base = v * seq
        for peer in range(base // own, (base + seq) // own):
            first = peer * own - base
            rows = taken[first : first + own]
            out_ref[peer] = jnp.concatenate([rows[:, :half], rows[:, half:]], axis=0)


def unpack(rows, own):
    packs = rows.shape[0] // (2 * own)
    token = lax.broadcasted_iota(jnp.int32, (packs * own, rows.shape[0]), 0)
    source = lax.broadcasted_iota(jnp.int32, (packs * own, rows.shape[0]), 1)
    first = (token // own) * (2 * own) + token % own
    low = dot32(jnp.where(source == first, 1.0, 0.0).astype(BF16), rows)
    high = dot32(jnp.where(source == first + own, 1.0, 0.0).astype(BF16), rows)
    return low, high


def attend_kernel(index_ref, rows_ref, w_qkv_ref, w_out_ref, out_ref):
    frames, packed, half = rows_ref.shape
    own = packed // 2
    width = 2 * half
    seq = frames * TOKL
    videos = frames * own // seq
    low, high = unpack(rows_ref[...].reshape(frames * packed, half), own)
    raw = jnp.concatenate([low, high], axis=1)
    centred = raw - jnp.mean(raw, axis=1, keepdims=True)
    variance = jnp.mean(centred * centred, axis=1, keepdims=True)
    normed = (centred * lax.rsqrt(variance + NORM_EPS)).astype(BF16)

    pairs = frames * own // packed

    def project(start):
        part = dot32(normed, w_qkv_ref[:, start : start + width])
        return part.astype(BF16).astype(F32).reshape(pairs, packed, width)

    table = index_ref[...].astype(F32)
    row = lax.broadcasted_iota(jnp.int32, (1, packed, LANES), 1)
    upper = row >= own
    me = table[:1, :1, KMAX + 1 : KMAX + 2].astype(jnp.int32)
    flat = me * own + jnp.where(upper, row - own, row)
    owner = jnp.zeros((pairs, packed, LANES), F32)
    for v in range(videos):
        count = table[:, v : v + 1, KMAX : KMAX + 1]
        upto = count
        step = 1
        while step < frames:
            moved = jnp.concatenate([jnp.zeros((step, 1, 1), F32), upto[:-step]], axis=0)
            upto = upto + moved
            step *= 2
        place = (flat - v * seq).astype(F32)
        ours = jnp.logical_and(flat >= v * seq, flat < (v + 1) * seq)
        below = upto - count
        below = below.reshape(pairs, 2, 1, 1)
        upto = upto.reshape(pairs, 2, 1, 1)
        start = jnp.where(upper, below[:, 1], below[:, 0])
        stop = jnp.where(upper, upto[:, 1], upto[:, 0])
        inside = jnp.logical_and(place >= start, place < stop)
        owner = owner + jnp.where(jnp.logical_and(inside, ours), 1.0, 0.0)
    owner = owner[:, :, :1]

    def over_frames(values):
        total = jnp.sum(values, axis=0)
        return total + swap_halves(total)

    query = over_frames(project(0) * owner)
    product = (project(width) * query[None]).reshape(-1, width)
    feature = lax.broadcasted_iota(jnp.int32, (width, LANES), 0) // HEAD_DIM
    head = lax.broadcasted_iota(jnp.int32, (width, LANES), 1)
    to_head = jnp.where(feature == head, 1.0, 0.0).astype(BF16)
    coarse = product.astype(BF16)
    rest = product - coarse.astype(F32)
    fine = rest.astype(BF16)
    last = (rest - fine.astype(F32)).astype(BF16)
    scores = dot32(jnp.concatenate([coarse, fine, last], axis=0), to_head)
    scores = jnp.sum(scores.reshape(3, pairs, packed, LANES), axis=0) * SCORE_SCALE
    largest = jnp.max(scores, axis=0)
    largest = jnp.maximum(largest, swap_halves(largest))
    raised = jnp.exp(scores - largest[None])
    weights = (raised / over_frames(raised)[None]).astype(BF16)
    head = lax.broadcasted_iota(jnp.int32, (LANES, width), 0)
    feature = lax.broadcasted_iota(jnp.int32, (LANES, width), 1) // HEAD_DIM
    from_head = jnp.where(feature == head, 1.0, 0.0).astype(BF16)
    spread = dot32(weights.reshape(-1, LANES), from_head).reshape(pairs, packed, width)
    attended = over_frames(spread * project(2 * width)).astype(BF16)
    change = dot32(attended, w_out_ref[...])
    residual = over_frames(raw.reshape(pairs, packed, width) * owner)
    encoded = residual + change
    place = lax.broadcasted_iota(jnp.int32, (packed, half), 0)
    encoded = jnp.where(place < own, encoded[:, :half], encoded[:, half:]).astype(BF16)
    out_ref[...] = jnp.broadcast_to(encoded[None], out_ref.shape)


def project_kernel(rows_ref, w_proj_ref, gain_ref, out_ref):
    frames, packed, half = rows_ref.shape
    own = packed // 2
    rows = rows_ref[...].reshape(frames * packed, half)
    low, high = (part.astype(BF16) for part in unpack(rows, own))
    total = dot32(low, w_proj_ref[:half, :]) + dot32(high, w_proj_ref[half:, :])
    gain = gain_ref[...].astype(F32)
    lanes = gain.shape[1]
    for r in range(gain.shape[0]):
        piece = slice(r * lanes, (r + 1) * lanes)
        gained = (total[:, piece] * gain[r : r + 1]).astype(BF16)
        out_ref[:, piece] = gained


def places(index_ref, sources):
    me = jnp.max(index_ref[0, :1, KMAX + 1 : KMAX + 2].astype(F32)).astype(jnp.int32)
    row = me // NEAR
    found = []
    for flip, steps, direct in sources:
        near = jnp.bitwise_xor(me - row * NEAR, flip)
        for i, step in enumerate(steps):
            outer = jnp.bitwise_xor(row, step) if direct else step
            found.append((i, outer * NEAR + near))
    return found


def square_sums(blocks, videos, index_ref):
    tokens, columns = blocks[0][0].shape[1:]
    gain_rows = -(-columns // LANES)
    squares = jnp.zeros((tokens, LANES), F32)
    for rows_ref, i, place in blocks:
        inverse = 1.0 / index_ref[place].astype(F32)[videos : videos + gain_rows]
        for r in range(gain_rows):
            piece = rows_ref[i, :, r * LANES : min((r + 1) * LANES, columns)].astype(F32)
            piece = piece * inverse[r : r + 1, : piece.shape[1]]
            piece = piece * piece
            if piece.shape[1] < LANES:
                fill = jnp.zeros((tokens, LANES - piece.shape[1]), F32)
                piece = jnp.concatenate([piece, fill], axis=1)
            squares = squares + piece
    return squares


def products(blocks, w_gate_ref, w_up_ref, begun, emit, limit):
    columns = blocks[0][0].shape[2]
    width = w_gate_ref.shape[1]
    block = min(width, limit)
    for first in range(0, width, block):
        sums = []
        for i, w_ref in enumerate((w_gate_ref, w_up_ref)):
            total = begun[i][:, first : first + block] if begun else None
            for rows_ref, part, place in blocks:
                depth = pl.ds(pl.multiple_of(place * columns, columns), columns)
                one = dot32(rows_ref[part], w_ref[depth, first : first + block])
                total = one if total is None else total + one
            sums.append(total)
        emit(first, block, *sums)


def split_refs(sources, refs):
    index_ref, w_gate_ref, w_up_ref = refs[:3]
    rows = refs[3 : 3 + len(sources)]
    owners = [ref for ref, source in zip(rows, sources) for _ in source[1]]
    blocks = [(ref,) + found for ref, found in zip(owners, places(index_ref, sources))]
    return index_ref, w_gate_ref, w_up_ref, blocks, refs[3 + len(sources) :]


def partial_kernel(sources, videos, *refs):
    index_ref, w_gate_ref, w_up_ref, blocks, rest = split_refs(sources, refs)
    begun, (gate_ref, up_ref, squares_ref) = rest[:-3], rest[-3:]

    def emit(first, block, gate, up):
        gate_ref[:, first : first + block] = gate
        up_ref[:, first : first + block] = up

    squares = square_sums(blocks, videos, index_ref)
    squares_ref[...] = squares + begun[2][...] if begun else squares
    products(blocks, w_gate_ref, w_up_ref, begun, emit, WIDE)


def final_kernel(sources, *refs):
    refs, (hidden_ref, sems) = refs[:-2], refs[-2:]
    index_ref, w_gate_ref, w_up_ref, blocks, rest = split_refs(sources, refs)
    begun, out_hbm = rest[:3], rest[3]
    videos = hidden_ref.shape[0]
    squares = begun[2][...] + square_sums(blocks, videos, index_ref)
    mean = jnp.sum(squares, axis=1, keepdims=True) / w_gate_ref.shape[0]
    scale = lax.rsqrt(mean + NORM_EPS)
    copies = []

    def emit(first, block, gate, up):
        hidden = (jax.nn.silu(gate * scale) * (up * scale)).astype(BF16)
        units = slice(first, first + block)
        hidden_ref[:, :, units] = hidden.reshape(videos, -1, block)
        copy = pltpu.make_async_copy(
            hidden_ref.at[:, :, units], out_hbm.at[:, :, units], sems.at[len(copies)]
        )
        copy.start()
        copies.append(copy)

    products(blocks, w_gate_ref, w_up_ref, begun, emit, BLOCK)
    for copy in copies:
        copy.wait()


def program(video, w_qkv, w_out, keep_list, kept_counts, w_proj, llm_gain, w_gate, w_up):
    videos, _, patches, width = video.shape
    axes = ("outer", "mid", "cores")
    frames, outer = lax.axis_size(axes), lax.axis_size("outer")
    seq = frames * TOKL
    tokens = videos * seq
    packed = 2 * (tokens // frames)
    half = width // 2
    columns = w_proj.shape[1]
    spread = functools.partial(lax.all_to_all, split_axis=0, concat_axis=0, tiled=True)
    gain_rows = -(-columns // LANES)
    gain = llm_gain.reshape(gain_rows, -1)

    counts, listed = kept_counts.T, keep_list
    kind = BF16 if max(patches, frames) <= 256 else F32
    rows = -(-(videos + gain_rows) // 8) * 8
    message = pl.pallas_call(
        index_kernel,
        out_shape=jax.ShapeDtypeStruct((frames, rows, LANES), kind),
        in_specs=[whole(pltpu.HBM)] * 3,
        out_specs=whole(),
        scratch_shapes=[pltpu.VMEM(x.shape, x.dtype) for x in (counts, listed, gain)]
        + [pltpu.SemaphoreType.DMA((3,))],
        compiler_params=params(2 * MIB),
        cost_estimate=pl.CostEstimate(flops=COVER_FLOPS, bytes_accessed=65536, transcendentals=0),
        name="index",
    )(*(pltpu.with_memory_space_constraint(x, pltpu.HBM) for x in (counts, listed, gain)))
    index = spread(message, axes)

    chosen = pl.pallas_call(
        select_kernel,
        out_shape=jax.ShapeDtypeStruct((frames, packed, half), BF16),
        in_specs=[whole(), whole()],
        out_specs=whole(),
        compiler_params=params(3 * MIB + 8 * tokens * width),
        name="select",
    )(index, video)
    seen = spread(chosen, axes)

    encoded = pl.pallas_call(
        attend_kernel,
        out_shape=jax.ShapeDtypeStruct((frames, packed, half), BF16),
        in_specs=[whole()] * 4,
        out_specs=whole(),
        compiler_params=params(4 * MIB + 24 * frames * packed * width),
        name="attend",
    )(index, seen, w_qkv, w_out)
    token_rows = spread(encoded, axes)

    gained = pl.pallas_call(
        project_kernel,
        out_shape=jax.ShapeDtypeStruct((tokens, columns), BF16),
        in_specs=[whole(), whole(), whole()],
        out_specs=whole(),
        compiler_params=params(4 * MIB + 16 * tokens * columns),
        name="project",
    )(token_rows, w_proj, gain)

    def swap(values, axis, flip=1):
        pairs = [(i, i ^ flip) for i in range(lax.axis_size(axis))]
        return lax.ppermute(values, axis, pairs)

    units = w_gate.shape[1]
    part = jax.ShapeDtypeStruct((tokens, units), F32)
    sums = (part, part, jax.ShapeDtypeStruct((tokens, LANES), F32))
    work = pl.CostEstimate(
        flops=tokens * w_gate.shape[0] * units // 2,
        bytes_accessed=w_gate.shape[0] * units // 2,
        transcendentals=0,
    )

    direct = outer == DIRECT
    if direct:
        blocks = [gained] + [swap(gained, "outer", k) for k in range(1, outer)]
        near, rest = jnp.stack(blocks[:2]), jnp.stack(blocks[2:])
        mid0, mid1 = swap(near, "mid"), swap(rest, "mid")
        core0, core1 = swap(near, "cores"), swap(rest, "cores")
        both0, both1 = swap(mid0, "cores"), swap(mid1, "cores")
        first, second = (0, 1), (2, 3)
        stages = (
            ((near, 0, first),),
            ((core0, 1, first),),
            ((rest, 0, second),),
            ((core1, 1, second), (mid0, 2, first),),
            ((both0, 3, first),),
            ((mid1, 2, second),),
            ((both1, 3, second),),
        )
    else:
        line = spread(jnp.broadcast_to(gained[None], (outer,) + gained.shape), "outer")
        steps = tuple(range(outer))
        mid = swap(line, "mid")
        core, both = swap(line, "cores"), swap(mid, "cores")
        blocks = ((line, 0), (core, 1), (mid, 2), (both, 3))
        stages = tuple(((block, flip, steps),) for block, flip in blocks)
    begun = ()
    for i, stage in enumerate(stages):
        sources = tuple((flip, steps, direct) for _, flip, steps in stage)
        last = i + 1 == len(stages)
        begun = pl.pallas_call(
            functools.partial(final_kernel, sources)
            if last
            else functools.partial(partial_kernel, sources, videos),
            out_shape=jax.ShapeDtypeStruct((videos, seq, units), BF16) if last else sums,
            in_specs=[whole()] * (3 + len(stage) + len(begun)),
            out_specs=whole(pl.ANY) if last else (whole(),) * 3,
            scratch_shapes=[
                pltpu.VMEM((videos, seq, units), BF16),
                pltpu.SemaphoreType.DMA((-(-units // BLOCK),)),
            ]
            if last
            else [],
            compiler_params=params(3 * MIB + 20 * tokens * units),
            cost_estimate=work,
            name="final" if last else "part",
        )(index, w_gate, w_up, *(block for block, _, _ in stage), *begun)
    return begun


def solution(mesh):
    groups, frames = mesh.devices.shape
    devices = mesh.devices.reshape(groups, frames // 4, 2, 2)
    split = Mesh(devices, ("groups", "outer", "mid", "cores"))
    spread = ("outer", "mid", "cores")
    in_specs = (
        P("groups", spread, None, None),
        P(),
        P(),
        P("groups", spread, None),
        P("groups", spread),
        P(None, spread),
        P(spread),
        P(None, spread),
        P(None, spread),
    )
    out_specs = P("groups", None, spread)
    return jax.shard_map(
        program, mesh=split, in_specs=in_specs, out_specs=out_specs, check_vma=False
    )
```
